256 devices in a mesh: sec: 64 (over z, x, core), row: 4 (over y).
Axes of the slice: x: 4, y: 4, z: 8, core: 2. Of those that a mesh axis runs over, the one named last changes fastest.
Arguments:
- left_block: bfloat16 [128, 2048, 128], P('sec', 'row'), may hold values from -6 to 6
- right_block: bfloat16 [128, 128, 2048], P('sec'), may hold values from -6 to 6
- left_ops: float32 [4, 16, 16], replicated, may hold values from -1.5 to 1.5
- right_ops: float32 [4, 16, 16], replicated, may hold values from -1.5 to 1.5
- charges: int32 [128], replicated, may hold values from 0 to 6
- live_states: int32 [128], replicated, may hold values from 64 to 128
- kept: int32 [128], replicated, may hold values from 64 to 128
- start: int32 [128, 128], replicated, may hold values from 0 to 511, all different within a row
Outputs:
- basis: float32 [128, 2048, 128], P('sec', 'row')
- right_new: float32 [128, 128, 2048], P('sec', None, 'row')
The draws below stay inside these ranges and needn't reach their ends.
Inputs may be any that keep to these rules, and one draw needn't show every extreme that they name: The 128 start columns of a sector are distinct.
All inputs are finite; a program needn't handle non-finite values.
Results may differ from the reference program's by a relative error of at most 0.0065.
Values may be sent and summed in bfloat16 or wider, within the bound.
No kernel may reach another device: no remote copies, remote signals or barrier semaphores. Data moves between devices by JAX's collectives and lax.ppermute only.
A program may use at most 64 MiB of HBM per device.

```python
import jax
import jax.numpy as jnp
from jax import lax

SITE = 16
STATES = 128
KEEP = 128
TERMS = 4
ITERS = 2
SECTORS = 128
ROWS = 2048
COLS = 2048


def set_ends(result, stream_key, least, top_value):
    place = [jax.random.randint(jax.random.fold_in(stream_key, axis), (), 0, length) for axis, length in enumerate(result.shape)]
    widest = result.shape.index(max(result.shape))
    neighbour = place[:widest] + [(place[widest] + 1) % result.shape[widest]] + place[widest + 1:]
    return result.at[tuple(place)].set(least).at[tuple(neighbour)].set(top_value)


def levels(stream_key, shape, shards, smallest, largest):
    factor_of, own = 1.0, jax.random.fold_in(stream_key, 6)
    for dim, shards_of in shards:
        draws = jnp.exp(jax.random.uniform(jax.random.fold_in(own, dim), (shards_of,), jnp.float32, smallest / len(shards), largest / len(shards)))
        factor_of = factor_of * jnp.repeat(draws, shape[dim] // shards_of).reshape([-1 if axis == dim else 1 for axis in range(len(shape))])
    return factor_of


def different_ones(stream_key, rows, count, top, lift):
    ranking = jax.random.permutation(jax.random.fold_in(stream_key, 1), count)
    favour = ranking
    for power in range(3):
        favour = favour * favour // count
    favour = favour * lift // count
    tickets = jax.random.randint(jax.random.fold_in(stream_key, 2), (rows, count), 0, 4096) + favour
    holders = jax.random.permutation(jax.random.fold_in(stream_key, 3), rows)[jnp.arange(count) % rows]
    tickets = jnp.where(jnp.arange(rows)[:, None] == holders[None, :], 1 << 14, tickets)
    score = tickets * count + jnp.arange(count)
    return lax.top_k(score.astype(jnp.int32), top)[1].astype(jnp.int32)


def noise(own_key, shape, spread, reach, shards=(), kind=jnp.bfloat16):
    factor_of = levels(own_key, shape, shards, -0.22, 0.18) if shards else 1.0
    values = jax.random.normal(own_key, shape, jnp.float32) * spread * factor_of
    return jnp.minimum(jnp.maximum(values, -reach), reach).astype(kind)


def setup_inputs(seed: int = 0) -> dict:
    keys = jax.random.split(jax.random.key(seed), 9)
    return {
        "left_block": noise(keys[0], (SECTORS, ROWS, STATES), 1.0, 6.0, ((0, 64), (1, 4))),
        "right_block": noise(keys[1], (SECTORS, STATES, COLS), 1.0, 6.0, ((0, 64),)),
        "left_ops": noise(keys[2], (TERMS, SITE, SITE), SITE ** -0.5, 1.5, (), jnp.float32),
        "right_ops": noise(keys[3], (TERMS, SITE, SITE), SITE ** -0.5, 1.5, (), jnp.float32),
        "charges": set_ends(jax.random.randint(keys[4], (SECTORS,), 0, 7), jax.random.fold_in(keys[4], 1), 0, 6).astype(jnp.int32),
        "live_states": set_ends(jax.random.randint(keys[5], (SECTORS,), STATES // 2, STATES + 1), jax.random.fold_in(keys[5], 1), STATES // 2, STATES).astype(jnp.int32),
        "kept": set_ends(jax.random.randint(keys[6], (SECTORS,), KEEP // 2, KEEP + 1), jax.random.fold_in(keys[6], 1), KEEP // 2, KEEP).astype(jnp.int32),
        "start": different_ones(keys[7], SECTORS, TERMS * STATES, KEEP, 0),
    }


chemical = 0.4
highest = lax.Precision.HIGHEST

def gate_rows(tensor_block, operators):
    site_dim = operators.shape[1]
    grouped = tensor_block.astype(jnp.float32).reshape(tensor_block.shape[0] // site_dim, site_dim, tensor_block.shape[1])
    mixed_rows = jnp.einsum('tij,ajk->aitk', operators.astype(jnp.float32), grouped, precision=highest)
    return mixed_rows.reshape(tensor_block.shape[0], operators.shape[0] * tensor_block.shape[1]).astype(jnp.bfloat16)

def gate_columns(tensor_block, operators):
    site_dim = operators.shape[1]
    grouped = tensor_block.astype(jnp.float32).reshape(tensor_block.shape[0], site_dim, tensor_block.shape[1] // site_dim)
    mixed_columns = jnp.einsum('tij,kjb->tkib', operators.astype(jnp.float32), grouped, precision=highest)
    return mixed_columns.reshape(operators.shape[0] * tensor_block.shape[0], tensor_block.shape[1]).astype(jnp.bfloat16)

def orthonormal(krylov):
    gram_matrix = jnp.dot(krylov.T, krylov, precision=highest)
    factor = jnp.linalg.cholesky(gram_matrix)
    return jax.scipy.linalg.solve_triangular(factor, krylov.T, lower=True).T

def reference(left_block, right_block, left_ops, right_ops, charges, live_states, kept, start):
    half_count = SECTORS // 2

    def one_sector(packed):
        left_tensor, right_tensor, live_count, charge_value, kept_count, columns = packed
        row_states = jnp.arange(left_tensor.shape[0], dtype=jnp.int32) // SITE
        left_masked = jnp.where((row_states < live_count)[:, None], left_tensor, jnp.zeros((), jnp.bfloat16))
        left_gated = gate_rows(left_masked, left_ops)
        right_gated = gate_columns(right_tensor, right_ops)
        weight = jnp.exp(-chemical * charge_value.astype(jnp.float32))
        theta_block = weight * jnp.dot(left_gated.astype(jnp.float32), right_gated.astype(jnp.float32), preferred_element_type=jnp.float32)
        krylov = jnp.take(left_gated, columns, axis=1).astype(jnp.float32)
        for round_index in range(ITERS):
            ortho_block = orthonormal(krylov)
            projected = jnp.dot(theta_block.T, ortho_block, precision=highest)
            krylov = jnp.dot(theta_block, projected, precision=highest)
        ortho_block = orthonormal(krylov)
        right_part = jnp.dot(ortho_block.T, theta_block, precision=highest)
        keep_mask = (jnp.arange(KEEP, dtype=jnp.int32) < kept_count).astype(jnp.float32)
        return (ortho_block * keep_mask[None, :], right_part * keep_mask[:, None])
    paired = (left_block, jnp.roll(right_block, -half_count, axis=0), live_states, jnp.roll(charges, -half_count), jnp.roll(kept, -half_count), start)
    basis_all, right_all = lax.map(one_sector, paired)
    total_weight = jnp.sum(right_all * right_all)
    right_all = right_all / jnp.sqrt(total_weight)
    return (basis_all, jnp.roll(right_all, half_count, axis=0))
```

```python
import functools

import jax
import jax.numpy as jnp
from jax import lax
from jax.experimental import pallas as pl
from jax.experimental.pallas import tpu as pltpu
from jax.sharding import Mesh
from jax.sharding import PartitionSpec as P

SITE = 16
ITERS = 2
SEC = ("sec_0", "sec_1", "sec_2")
SEC_ROW = ("sec_0", "sec_1", "sec_2", "row")
WINDOW = 32

chemical = 0.4
highest = lax.Precision.HIGHEST


def from_partner(value, axis, distance):
    mask = 2**distance
    pairs = [(source, source ^ mask) for source in range(lax.axis_size(axis))]
    return lax.ppermute(value, axis, pairs)


def dot_over(left, right, left_dim, right_dim, precision=None):
    return lax.dot_general(
        left,
        right,
        (((left_dim,), (right_dim,)), ((), ())),
        precision=precision,
        preferred_element_type=jnp.float32,
    )


def two_parts(values):
    high = values.astype(jnp.bfloat16)
    low = (values - high.astype(jnp.float32)).astype(jnp.bfloat16)
    return high, low


def one_hot(shape, row_key, col_key):
    rows = lax.broadcasted_iota(jnp.int32, shape, 0)
    cols = lax.broadcasted_iota(jnp.int32, shape, 1)
    return row_key(rows) == col_key(cols)


def as_weights(mask):
    return jnp.where(mask, 1.0, 0.0).astype(jnp.bfloat16)


def lower_inverse(grams, window):
    n = grams[0].shape[0]
    lane = lax.broadcasted_iota(jnp.int32, (8, n), 1)
    sub = lax.broadcasted_iota(jnp.int32, (8, n), 0)
    rows = [[g[8 * q : 8 * q + 8, :] for q in range(n // 8)] for g in grams]
    span = window // 8
    for first in range(0, n // 8, span):
        last = first + span
        for q in range(first, last):
            k = 8 * q
            inside = (lane >= k) & (lane < k + 8)
            unit = (lane - k == sub).astype(jnp.float32)
            for mat in rows:
                cols = {
                    r: [jnp.broadcast_to(mat[r][:, k + m : k + m + 1], (8, n)) for m in range(8)]
                    for r in range(q, last)
                }
                for r in range(q, last):
                    mat[r] = jnp.where(inside, unit if r == q else 0.0, mat[r])
                for m in range(8):
                    pivot = jnp.broadcast_to(cols[q][m][m : m + 1, :], (8, n))
                    scale = lax.rsqrt(pivot)
                    head = jnp.broadcast_to(mat[q][m : m + 1, :], (8, n)) * scale
                    below = {r: cols[r][m] * scale for r in range(q, last)}
                    below[q] = jnp.where(sub > m, below[q], 0.0)
                    for j in range(m + 1, 8):
                        weight = jnp.broadcast_to(below[q][j : j + 1, :], (8, n))
                        for r in range(q, last):
                            cols[r][j] = cols[r][j] - below[r] * weight
                    for r in range(q, last):
                        mat[r] = mat[r] - below[r] * head
                    mat[q] = jnp.where(sub == m, head, mat[q])
        if last < n // 8:
            inblock = (lane >= 8 * first) & (lane < 8 * last)
            for mat in rows:
                panel = jnp.concatenate(mat[first:last], axis=0)
                panel_row = lax.broadcasted_iota(jnp.int32, panel.shape, 0) + 8 * first
                panel_lane = lax.broadcasted_iota(jnp.int32, panel.shape, 1)
                panel = jnp.where((panel_lane > panel_row) & (panel_lane < 8 * last), 0.0, panel)
                update = dot_over(panel, panel, 0, 0, highest)
                for r in range(last, n // 8):
                    mat[r] = jnp.where(inblock, 0.0, mat[r]) - update[8 * r : 8 * r + 8, :]
    full_row = lax.broadcasted_iota(jnp.int32, (n, n), 0)
    full_col = lax.broadcasted_iota(jnp.int32, (n, n), 1)
    return [jnp.where(full_col <= full_row, jnp.concatenate(mat, axis=0), 0.0) for mat in rows]


def right_kernel(
    row_ref, right_ref, right_ops_ref, left_ops_ref,
    square_ref, local_ref, left_mix_ref,
    right_mix, gated,
):
    terms, site = left_ops_ref.shape[0], SITE
    states = right_ref.shape[1]
    wide = site * site
    local_cols = local_ref.shape[2]

    @pl.when(pl.program_id(0) == 0)
    def _():
        spread = as_weights(
            one_hot((terms * wide, terms * site), lambda r: r // site, lambda c: c)
        )
        widen = as_weights(one_hot((site, wide), lambda r: r, lambda c: c // site))
        same = one_hot((terms * wide, wide), lambda r: r % site, lambda c: c % site)
        for part, piece in enumerate(two_parts(right_ops_ref[...])):
            tall = dot_over(spread, piece, 1, 0).astype(jnp.bfloat16)
            full = dot_over(tall, widen, 1, 0)
            right_mix[part] = jnp.where(same, full, 0.0).astype(jnp.bfloat16)
        tall_pick = as_weights(one_hot((wide, site), lambda r: r % site, lambda c: c))
        wide_pick = as_weights(one_hot((site, wide), lambda r: r, lambda c: c % site))
        group = one_hot((wide, wide), lambda r: r // site, lambda c: c // site)
        for t in range(terms):
            for part, piece in enumerate(two_parts(left_ops_ref[t])):
                tall = dot_over(tall_pick, piece, 1, 1).astype(jnp.bfloat16)
                full = dot_over(tall, wide_pick, 1, 0)
                left_mix_ref[t, part] = jnp.where(group, full, 0.0).astype(jnp.bfloat16)

    for pair in range(states // (2 * site)):
        base = pair * 2 * site
        halves = [
            jnp.concatenate(
                [
                    right_ref[0, base + h * site : base + (h + 1) * site, j * states : (j + 1) * states]
                    for j in range(site)
                ],
                axis=0,
            )
            for h in range(2)
        ]
        block = jnp.concatenate(halves, axis=1)
        for t in range(terms):
            rows = pl.ds(t * wide, wide)
            mixed = dot_over(right_mix[0, rows, :], block, 1, 0) + dot_over(
                right_mix[1, rows, :], block, 1, 0
            )
            mixed = mixed.astype(jnp.bfloat16)
            for h in range(2):
                for i in range(site):
                    gated[
                        t * states + base + h * site : t * states + base + (h + 1) * site,
                        i * states : (i + 1) * states,
                    ] = mixed[i * site : (i + 1) * site, h * states : (h + 1) * states]
    square_ref[0] = dot_over(gated[...], gated[...], 1, 1)
    offset = pl.multiple_of(row_ref[0] * local_cols, local_cols)
    local_ref[0] = gated[:, pl.ds(offset, local_cols)]


def krylov_kernel(
    row_ref, live_ref, kept_ref, weight_ref, left_ref, left_mix_ref, square_ref, local_ref, start_ref,
    basis_ref, right_ref, total_ref,
    gated, gram, block, image,
):
    chunks, slots, chunk_rows, states = left_ref.shape
    terms = left_mix_ref.shape[0]
    wide = left_mix_ref.shape[2]
    keep = block.shape[1]
    for s in range(slots):
        pieces = []
        for c in range(chunks):
            turned = left_ref[c, s].T
            for b in range(chunk_rows // wide):
                lane = lax.broadcasted_iota(jnp.int32, (states, wide), 1)
                alive = lane < live_ref[s] * SITE - (c * chunk_rows + b * wide)
                piece = turned[:, b * wide : (b + 1) * wide].astype(jnp.float32)
                pieces.append(jnp.where(alive, piece, 0.0).astype(jnp.bfloat16))
        tall = jnp.concatenate(pieces, axis=0)
        for t in range(terms):
            mixed = dot_over(tall, left_mix_ref[t, 0], 1, 0) + dot_over(
                tall, left_mix_ref[t, 1], 1, 0
            )
            mixed = mixed.astype(jnp.bfloat16)
            for b in range(len(pieces)):
                gated[s, t * states : (t + 1) * states, b * wide : (b + 1) * wide] = mixed[
                    b * states : (b + 1) * states, :
                ]
        gram[s] = dot_over(gated[s], gated[s], 1, 1)
        spots = lax.broadcasted_iota(jnp.int32, (keep, terms * states), 1)
        block[s] = jnp.where(spots == start_ref[s], 1.0, 0.0)

    def step(index, carry):
        images = [dot_over(block[s], gram[s], 1, 0, highest) for s in range(slots)]
        grams = [dot_over(images[s], block[s], 1, 1, highest) for s in range(slots)]
        inverses = lower_inverse(grams, WINDOW)
        for s in range(slots):
            image[s] = dot_over(inverses[s], images[s], 1, 0, highest)

        @pl.when(index < ITERS)
        def _():
            for s in range(slots):
                scale = weight_ref[s] * weight_ref[s]
                block[s] = scale * dot_over(image[s], square_ref[s], 1, 0, highest)

        @pl.when(index == ITERS)
        def _():
            for s in range(slots):
                block[s] = dot_over(inverses[s], block[s], 1, 0, highest)

        return carry

    lax.fori_loop(0, ITERS + 1, step, 0)
    offset = pl.multiple_of(row_ref[0] * chunk_rows, chunk_rows)
    total = jnp.zeros((1, 1), jnp.float32)
    for s in range(slots):
        mine = gated[s, :, pl.ds(offset, chunk_rows)]
        high, low = two_parts(block[s])
        basis = dot_over(high, mine, 1, 0) + dot_over(low, mine, 1, 0)
        keeps = lax.broadcasted_iota(jnp.int32, basis.shape, 0) < kept_ref[s]
        basis_ref[s] = jnp.where(keeps, basis, 0.0).T.astype(jnp.bfloat16)
        high, low = two_parts(image[s])
        part = dot_over(high, local_ref[s], 1, 0) + dot_over(low, local_ref[s], 1, 0)
        keeps = lax.broadcasted_iota(jnp.int32, part.shape, 0) < kept_ref[s]
        part = jnp.where(keeps, part * weight_ref[s], 0.0)
        right_ref[s] = part
        total += jnp.sum(jnp.sum(part * part, axis=0, keepdims=True), axis=1, keepdims=True)
    total_ref[...] = total


def smem():
    return pl.BlockSpec(memory_space=pltpu.SMEM)


def vmem():
    return pl.BlockSpec(memory_space=pltpu.VMEM)


def whole(shape):
    return pl.BlockSpec(shape, lambda s: (0,) * len(shape))


def slot(shape):
    return pl.BlockSpec((1, *shape), lambda s: (s,) + (0,) * len(shape))


def gate_right(row, right_block, right_ops, left_ops, local_cols):
    slots, states, cols = right_block.shape
    terms = left_ops.shape[0]
    bond, wide = terms * states, SITE * SITE
    return pl.pallas_call(
        right_kernel,
        grid=(slots,),
        in_specs=[smem(), slot((states, cols)), whole((terms * SITE, SITE)), whole(left_ops.shape)],
        out_specs=[
            slot((bond, bond)),
            slot((bond, local_cols)),
            whole((terms, 2, wide, wide)),
        ],
        out_shape=[
            jax.ShapeDtypeStruct((slots, bond, bond), jnp.float32),
            jax.ShapeDtypeStruct((slots, bond, local_cols), jnp.bfloat16),
            jax.ShapeDtypeStruct((terms, 2, wide, wide), jnp.bfloat16),
        ],
        scratch_shapes=[
            pltpu.VMEM((2, terms * wide, wide), jnp.bfloat16),
            pltpu.VMEM((bond, cols), jnp.bfloat16),
        ],
        compiler_params=pltpu.CompilerParams(vmem_limit_bytes=40 << 20),
        cost_estimate=pl.CostEstimate(flops=int(1e10), bytes_accessed=6 << 20, transcendentals=0),
        name="right_gate",
    )(row, right_block, right_ops.reshape(terms * SITE, SITE), left_ops)


def krylov_part(row, live, kept, weight, left_all, left_mix, square, local, start):
    chunks, slots, chunk_rows, states = left_all.shape
    bond, local_cols = local.shape[1:]
    keep = start.shape[1]
    return pl.pallas_call(
        krylov_kernel,
        in_specs=[smem()] * 4 + [vmem()] * 5,
        out_specs=[vmem()] * 3,
        out_shape=[
            jax.ShapeDtypeStruct((slots, chunk_rows, keep), jnp.bfloat16),
            jax.ShapeDtypeStruct((slots, keep, local_cols), jnp.float32),
            jax.ShapeDtypeStruct((1, 1), jnp.float32),
        ],
        scratch_shapes=[
            pltpu.VMEM((slots, bond, chunks * chunk_rows), jnp.bfloat16),
            pltpu.VMEM((slots, bond, bond), jnp.float32),
            pltpu.VMEM((slots, keep, bond), jnp.float32),
            pltpu.VMEM((slots, keep, bond), jnp.float32),
        ],
        compiler_params=pltpu.CompilerParams(vmem_limit_bytes=48 << 20),
        cost_estimate=pl.CostEstimate(flops=int(2e10), bytes_accessed=6 << 20, transcendentals=0),
        name="krylov",
    )(row, live, kept, weight, left_all, left_mix, square, local, start)


def on_device(left_block, right_block, left_ops, right_ops, charges, live_states, kept, start):
    slots = left_block.shape[0]
    sectors = slots * lax.axis_size(SEC)
    top_bit = lax.axis_size(SEC).bit_length() - 2
    right_first = lax.axis_index(SEC) * slots
    left_first = (right_first + sectors // 2) % sectors
    cut = lambda table, first: lax.dynamic_slice_in_dim(table, first, slots, 0)
    row = lax.axis_index("row").astype(jnp.int32).reshape(1)
    live = cut(live_states, left_first)
    kept_here = cut(kept, right_first)
    weight = jnp.exp(-chemical * cut(charges, right_first).astype(jnp.float32))
    start_here = cut(start, left_first)[:, :, None]
    left_theirs = from_partner(left_block, SEC, top_bit)
    left_all = lax.all_gather(left_theirs, "row", axis=0, tiled=False)
    local_cols = right_block.shape[2] // lax.axis_size("row")
    square, local, left_mix = gate_right(row, right_block, right_ops, left_ops, local_cols)
    basis, right_part, total = krylov_part(
        row, live, kept_here, weight, left_all, left_mix, square, local, start_here
    )
    basis = from_partner(basis, SEC, top_bit).astype(jnp.float32)
    total = lax.psum(total[0, 0], SEC_ROW)
    return basis, right_part / jnp.sqrt(total)


def solution(mesh):
    finer = Mesh(
        mesh.devices.reshape(8, 4, 2, mesh.shape["row"]), ("sec_0", "sec_1", "sec_2", "row")
    )
    in_specs = (P(SEC, "row", None), P(SEC, None, None), P(), P(), P(), P(), P(), P())
    out_specs = (P(SEC, "row", None), P(SEC, None, "row"))
    return jax.shard_map(
        on_device, mesh=finer, in_specs=in_specs, out_specs=out_specs, check_vma=False
    )
```

```python
import functools

import jax
import jax.numpy as jnp
from jax import lax
from jax.experimental import pallas as pl
from jax.experimental.pallas import tpu as pltpu
from jax.sharding import Mesh
from jax.sharding import PartitionSpec as P

SITE = 16
ITERS = 2
SEC = ("sec_0", "sec_1", "sec_2")
SEC_ROW = ("sec_0", "sec_1", "sec_2", "row")
WINDOW = 32

chemical = 0.4
highest = lax.Precision.HIGHEST


def from_partner(value, axis, distance):
    mask = 2**distance
    pairs = [(source, source ^ mask) for source in range(lax.axis_size(axis))]
    return lax.ppermute(value, axis, pairs)


def dot_over(left, right, left_dim, right_dim, precision=None):
    return lax.dot_general(
        left,
        right,
        (((left_dim,), (right_dim,)), ((), ())),
        precision=precision,
        preferred_element_type=jnp.float32,
    )


def two_parts(values):
    high = values.astype(jnp.bfloat16)
    low = (values - high.astype(jnp.float32)).astype(jnp.bfloat16)
    return high, low


def one_hot(shape, row_key, col_key):
    rows = lax.broadcasted_iota(jnp.int32, shape, 0)
    cols = lax.broadcasted_iota(jnp.int32, shape, 1)
    return row_key(rows) == col_key(cols)


def as_weights(mask):
    return jnp.where(mask, 1.0, 0.0).astype(jnp.bfloat16)


def lower_inverse(grams, window):
    n = grams[0].shape[0]
    lane = lax.broadcasted_iota(jnp.int32, (8, n), 1)
    sub = lax.broadcasted_iota(jnp.int32, (8, n), 0)
    rows = [[g[8 * q : 8 * q + 8, :] for q in range(n // 8)] for g in grams]
    span = window // 8
    for first in range(0, n // 8, span):
        last = first + span
        for q in range(first, last):
            k = 8 * q
            inside = (lane >= k) & (lane < k + 8)
            unit = (lane - k == sub).astype(jnp.float32)
            for mat in rows:
                cols = {
                    r: [jnp.broadcast_to(mat[r][:, k + m : k + m + 1], (8, n)) for m in range(8)]
                    for r in range(q, last)
                }
                for r in range(q, last):
                    mat[r] = jnp.where(inside, unit if r == q else 0.0, mat[r])
                for m in range(8):
                    pivot = jnp.broadcast_to(cols[q][m][m : m + 1, :], (8, n))
                    scale = lax.rsqrt(pivot)
                    head = jnp.broadcast_to(mat[q][m : m + 1, :], (8, n)) * scale
                    below = {r: cols[r][m] * scale for r in range(q, last)}
                    below[q] = jnp.where(sub > m, below[q], 0.0)
                    for j in range(m + 1, 8):
                        weight = jnp.broadcast_to(below[q][j : j + 1, :], (8, n))
                        for r in range(q, last):
                            cols[r][j] = cols[r][j] - below[r] * weight
                    for r in range(q, last):
                        mat[r] = mat[r] - below[r] * head
                    mat[q] = jnp.where(sub == m, head, mat[q])
        if last < n // 8:
            inblock = (lane >= 8 * first) & (lane < 8 * last)
            for mat in rows:
                panel = jnp.concatenate(mat[first:last], axis=0)
                panel_row = lax.broadcasted_iota(jnp.int32, panel.shape, 0) + 8 * first
                panel_lane = lax.broadcasted_iota(jnp.int32, panel.shape, 1)
                panel = jnp.where((panel_lane > panel_row) & (panel_lane < 8 * last), 0.0, panel)
                update = dot_over(panel, panel, 0, 0, highest)
                for r in range(last, n // 8):
                    mat[r] = jnp.where(inblock, 0.0, mat[r]) - update[8 * r : 8 * r + 8, :]
    full_row = lax.broadcasted_iota(jnp.int32, (n, n), 0)
    full_col = lax.broadcasted_iota(jnp.int32, (n, n), 1)
    return [jnp.where(full_col <= full_row, jnp.concatenate(mat, axis=0), 0.0) for mat in rows]


def right_kernel(
    row_ref, right_ref, right_ops_ref, left_ops_ref,
    square_ref, local_ref, left_mix_ref,
    right_mix, gated,
):
    terms, site = left_ops_ref.shape[0], SITE
    states = right_ref.shape[1]
    wide = site * site
    local_cols = local_ref.shape[2]

    @pl.when(pl.program_id(0) == 0)
    def _():
        spread = as_weights(
            one_hot((terms * wide, terms * site), lambda r: r // site, lambda c: c)
        )
        widen = as_weights(one_hot((site, wide), lambda r: r, lambda c: c // site))
        same = one_hot((terms * wide, wide), lambda r: r % site, lambda c: c % site)
        for part, piece in enumerate(two_parts(right_ops_ref[...])):
            tall = dot_over(spread, piece, 1, 0).astype(jnp.bfloat16)
            full = dot_over(tall, widen, 1, 0)
            right_mix[part] = jnp.where(same, full, 0.0).astype(jnp.bfloat16)
        tall_pick = as_weights(one_hot((wide, site), lambda r: r % site, lambda c: c))
        wide_pick = as_weights(one_hot((site, wide), lambda r: r, lambda c: c % site))
        group = one_hot((wide, wide), lambda r: r // site, lambda c: c // site)
        for t in range(terms):
            for part, piece in enumerate(two_parts(left_ops_ref[t])):
                tall = dot_over(tall_pick, piece, 1, 1).astype(jnp.bfloat16)
                full = dot_over(tall, wide_pick, 1, 0)
                left_mix_ref[t, part] = jnp.where(group, full, 0.0).astype(jnp.bfloat16)

    for pair in range(states // (2 * site)):
        base = pair * 2 * site
        halves = [
            jnp.concatenate(
                [
                    right_ref[0, base + h * site : base + (h + 1) * site, j * states : (j + 1) * states]
                    for j in range(site)
                ],
                axis=0,
            )
            for h in range(2)
        ]
        block = jnp.concatenate(halves, axis=1)
        for t in range(terms):
            rows = pl.ds(t * wide, wide)
            mixed = dot_over(right_mix[0, rows, :], block, 1, 0) + dot_over(
                right_mix[1, rows, :], block, 1, 0
            )
            mixed = mixed.astype(jnp.bfloat16)
            for h in range(2):
                for i in range(site):
                    gated[
                        t * states + base + h * site : t * states + base + (h + 1) * site,
                        i * states : (i + 1) * states,
                    ] = mixed[i * site : (i + 1) * site, h * states : (h + 1) * states]
    square_ref[0] = dot_over(gated[...], gated[...], 1, 1)
    offset = pl.multiple_of(row_ref[0] * local_cols, local_cols)
    local_ref[0] = gated[:, pl.ds(offset, local_cols)]


def krylov_kernel(row_ref, live_ref, kept_ref, weight_ref, *refs):
    chunks = len(refs) - 12
    left_refs = refs[:chunks]
    (left_mix_ref, square_ref, local_ref, start_ref) = refs[chunks : chunks + 4]
    (basis_ref, right_ref, total_ref) = refs[chunks + 4 : chunks + 7]
    (gated, gram, block, image, final) = refs[chunks + 7 :]
    slots, chunk_rows, states = left_refs[0].shape
    terms = left_mix_ref.shape[0]
    wide = left_mix_ref.shape[2]
    keep = block.shape[1]
    for s in range(slots):
        pieces = []
        for c in range(chunks):
            turned = left_refs[c][s].T
            first_row = lax.rem(row_ref[0] + (chunks - c), chunks) * chunk_rows
            for b in range(chunk_rows // wide):
                lane = lax.broadcasted_iota(jnp.int32, (states, wide), 1)
                alive = lane < live_ref[s] * SITE - (first_row + b * wide)
                piece = turned[:, b * wide : (b + 1) * wide].astype(jnp.float32)
                pieces.append(jnp.where(alive, piece, 0.0).astype(jnp.bfloat16))
        tall = jnp.concatenate(pieces, axis=0)
        for t in range(terms):
            mixed = dot_over(tall, left_mix_ref[t, 0], 1, 0) + dot_over(
                tall, left_mix_ref[t, 1], 1, 0
            )
            mixed = mixed.astype(jnp.bfloat16)
            for b in range(len(pieces)):
                gated[s, t * states : (t + 1) * states, b * wide : (b + 1) * wide] = mixed[
                    b * states : (b + 1) * states, :
                ]
        gram[s] = dot_over(gated[s], gated[s], 1, 1)
        spots = lax.broadcasted_iota(jnp.int32, (keep, terms * states), 1)
        block[s] = jnp.where(spots == start_ref[s], 1.0, 0.0)

    def step(index, carry):
        images = [dot_over(block[s], gram[s], 1, 0, highest) for s in range(slots)]
        grams = [dot_over(images[s], block[s], 1, 1, highest) for s in range(slots)]
        inverses = lower_inverse(grams, WINDOW)
        for s in range(slots):
            image[s] = dot_over(inverses[s], images[s], 1, 0, highest)

        @pl.when(index == ITERS)
        def _():
            for s in range(slots):
                final[s] = dot_over(inverses[s], block[s], 1, 0, highest)

        for s in range(slots):
            scale = weight_ref[s] * weight_ref[s]
            block[s] = scale * dot_over(image[s], square_ref[s], 1, 0, highest)
        return carry

    lax.fori_loop(0, ITERS + 1, step, 0)
    total = jnp.zeros((1, 1), jnp.float32)
    for s in range(slots):
        keeps = lax.broadcasted_iota(jnp.int32, block.shape[1:], 0) < kept_ref[s]
        squared = jnp.where(keeps, block[s] * image[s], 0.0)
        total += jnp.sum(jnp.sum(squared, axis=0, keepdims=True), axis=1, keepdims=True)
        high, low = two_parts(final[s])
        mine = gated[s, :, :chunk_rows]
        basis = dot_over(high, mine, 1, 0) + dot_over(low, mine, 1, 0)
        keeps = lax.broadcasted_iota(jnp.int32, basis.shape, 0) < kept_ref[s]
        basis_ref[s] = jnp.where(keeps, basis, 0.0).T.astype(jnp.bfloat16)
        high, low = two_parts(image[s])
        part = dot_over(high, local_ref[s], 1, 0) + dot_over(low, local_ref[s], 1, 0)
        keeps = lax.broadcasted_iota(jnp.int32, part.shape, 0) < kept_ref[s]
        right_ref[s] = jnp.where(keeps, part * weight_ref[s], 0.0)
    total_ref[...] = jnp.broadcast_to(total, total_ref.shape)


def smem():
    return pl.BlockSpec(memory_space=pltpu.SMEM)


def vmem():
    return pl.BlockSpec(memory_space=pltpu.VMEM)


def whole(shape):
    return pl.BlockSpec(shape, lambda s: (0,) * len(shape))


def slot(shape):
    return pl.BlockSpec((1, *shape), lambda s: (s,) + (0,) * len(shape))


def gate_right(row, right_block, right_ops, left_ops, local_cols):
    slots, states, cols = right_block.shape
    terms = left_ops.shape[0]
    bond, wide = terms * states, SITE * SITE
    return pl.pallas_call(
        right_kernel,
        grid=(slots,),
        in_specs=[smem(), slot((states, cols)), whole((terms * SITE, SITE)), whole(left_ops.shape)],
        out_specs=[
            slot((bond, bond)),
            slot((bond, local_cols)),
            whole((terms, 2, wide, wide)),
        ],
        out_shape=[
            jax.ShapeDtypeStruct((slots, bond, bond), jnp.float32),
            jax.ShapeDtypeStruct((slots, bond, local_cols), jnp.bfloat16),
            jax.ShapeDtypeStruct((terms, 2, wide, wide), jnp.bfloat16),
        ],
        scratch_shapes=[
            pltpu.VMEM((2, terms * wide, wide), jnp.bfloat16),
            pltpu.VMEM((bond, cols), jnp.bfloat16),
        ],
        compiler_params=pltpu.CompilerParams(vmem_limit_bytes=20 << 20),
        cost_estimate=pl.CostEstimate(flops=int(1e10), bytes_accessed=6 << 20, transcendentals=0),
        name="right_gate",
    )(row, right_block, right_ops.reshape(terms * SITE, SITE), left_ops)


def krylov_part(row, live, kept, weight, left_chunks, left_mix, square, local, start, peers):
    slots, chunk_rows, states = left_chunks[0].shape
    bond, local_cols = local.shape[1:]
    keep = start.shape[1]
    return pl.pallas_call(
        krylov_kernel,
        in_specs=[smem()] * 4 + [vmem()] * (len(left_chunks) + 4),
        out_specs=[vmem()] * 3,
        out_shape=[
            jax.ShapeDtypeStruct((slots, chunk_rows, keep), jnp.bfloat16),
            jax.ShapeDtypeStruct((slots, keep, local_cols), jnp.float32),
            jax.ShapeDtypeStruct((peers, keep), jnp.float32),
        ],
        scratch_shapes=[
            pltpu.VMEM((slots, bond, len(left_chunks) * chunk_rows), jnp.bfloat16),
            pltpu.VMEM((slots, bond, bond), jnp.float32),
            pltpu.VMEM((slots, keep, bond), jnp.float32),
            pltpu.VMEM((slots, keep, bond), jnp.float32),
            pltpu.VMEM((slots, keep, bond), jnp.float32),
        ],
        compiler_params=pltpu.CompilerParams(vmem_limit_bytes=24 << 20),
        cost_estimate=pl.CostEstimate(flops=int(2e10), bytes_accessed=6 << 20, transcendentals=0),
        name="krylov",
    )(row, live, kept, weight, *left_chunks, left_mix, square, local, start)


def on_device(left_block, right_block, left_ops, right_ops, charges, live_states, kept, start):
    slots = left_block.shape[0]
    sectors = slots * lax.axis_size(SEC)
    top_bit = lax.axis_size(SEC).bit_length() - 2
    right_first = lax.axis_index(SEC) * slots
    left_first = (right_first + sectors // 2) % sectors
    cut = lambda table, first: lax.dynamic_slice_in_dim(table, first, slots, 0)
    row = lax.axis_index("row").astype(jnp.int32).reshape(1)
    live = cut(live_states, left_first)
    kept_here = cut(kept, right_first)
    weight = jnp.exp(-chemical * cut(charges, right_first).astype(jnp.float32))
    start_here = cut(start, left_first)[:, :, None]
    left_theirs = from_partner(left_block, SEC, top_bit)
    local_cols = right_block.shape[2] // lax.axis_size("row")
    square, local, left_mix = gate_right(row, right_block, right_ops, left_ops, local_cols)
    left_theirs, square = lax.optimization_barrier((left_theirs, square))
    rows = lax.axis_size("row")
    left_chunks = [left_theirs] + [
        lax.ppermute(left_theirs, "row", [(i, (i + d) % rows) for i in range(rows)])
        for d in range(1, rows)
    ]
    basis, right_part, total = krylov_part(
        row, live, kept_here, weight, left_chunks, left_mix, square, local, start_here,
        lax.axis_size(SEC),
    )
    basis = from_partner(basis, SEC, top_bit)
    totals = lax.all_to_all(total, SEC, split_axis=0, concat_axis=0, tiled=True)
    total = jnp.sum(totals[:, 0])
    return basis.astype(jnp.float32), right_part / jnp.sqrt(total)


def solution(mesh):
    finer = Mesh(
        mesh.devices.reshape(8, 4, 2, mesh.shape["row"]), ("sec_0", "sec_1", "sec_2", "row")
    )
    in_specs = (P(SEC, "row", None), P(SEC, None, None), P(), P(), P(), P(), P(), P())
    out_specs = (P(SEC, "row", None), P(SEC, None, "row"))
    return jax.shard_map(
        on_device, mesh=finer, in_specs=in_specs, out_specs=out_specs, check_vma=False
    )
```

```python
import functools

import jax
import jax.numpy as jnp
from jax import lax
from jax.experimental import pallas as pl
from jax.experimental.pallas import tpu as pltpu
from jax.sharding import Mesh
from jax.sharding import PartitionSpec as P

SITE = 16
ITERS = 2
SEC = ("sec_0", "sec_1", "sec_2")
SEC_ROW = ("sec_0", "sec_1", "sec_2", "row")
WINDOW = 32

chemical = 0.4
highest = lax.Precision.HIGHEST


def from_partner(value, axis, distance):
    mask = 2**distance
    pairs = [(source, source ^ mask) for source in range(lax.axis_size(axis))]
    return lax.ppermute(value, axis, pairs)


def dot_over(left, right, left_dim, right_dim, precision=None):
    return lax.dot_general(
        left,
        right,
        (((left_dim,), (right_dim,)), ((), ())),
        precision=precision,
        preferred_element_type=jnp.float32,
    )


def two_parts(values):
    high = values.astype(jnp.bfloat16)
    low = (values - high.astype(jnp.float32)).astype(jnp.bfloat16)
    return high, low


def one_hot(shape, row_key, col_key):
    rows = lax.broadcasted_iota(jnp.int32, shape, 0)
    cols = lax.broadcasted_iota(jnp.int32, shape, 1)
    return row_key(rows) == col_key(cols)


def as_weights(mask):
    return jnp.where(mask, 1.0, 0.0).astype(jnp.bfloat16)


def lower_inverse(grams, window):
    n = grams[0].shape[0]
    lane = lax.broadcasted_iota(jnp.int32, (8, n), 1)
    sub = lax.broadcasted_iota(jnp.int32, (8, n), 0)
    rows = [[g[8 * q : 8 * q + 8, :] for q in range(n // 8)] for g in grams]
    span = window // 8
    for first in range(0, n // 8, span):
        last = first + span
        for q in range(first, last):
            k = 8 * q
            inside = (lane >= k) & (lane < k + 8)
            unit = (lane - k == sub).astype(jnp.float32)
            for mat in rows:
                cols = {
                    r: [jnp.broadcast_to(mat[r][:, k + m : k + m + 1], (8, n)) for m in range(8)]
                    for r in range(q, last)
                }
                for r in range(q, last):
                    mat[r] = jnp.where(inside, unit if r == q else 0.0, mat[r])
                for m in range(8):
                    pivot = jnp.broadcast_to(cols[q][m][m : m + 1, :], (8, n))
                    scale = lax.rsqrt(pivot)
                    head = jnp.broadcast_to(mat[q][m : m + 1, :], (8, n)) * scale
                    below = {r: cols[r][m] * scale for r in range(q, last)}
                    below[q] = jnp.where(sub > m, below[q], 0.0)
                    for j in range(m + 1, 8):
                        weight = jnp.broadcast_to(below[q][j : j + 1, :], (8, n))
                        for r in range(q, last):
                            cols[r][j] = cols[r][j] - below[r] * weight
                    for r in range(q, last):
                        mat[r] = mat[r] - below[r] * head
                    mat[q] = jnp.where(sub == m, head, mat[q])
        if last < n // 8:
            inblock = (lane >= 8 * first) & (lane < 8 * last)
            for mat in rows:
                panel = jnp.concatenate(mat[first:last], axis=0)
                panel_row = lax.broadcasted_iota(jnp.int32, panel.shape, 0) + 8 * first
                panel_lane = lax.broadcasted_iota(jnp.int32, panel.shape, 1)
                panel = jnp.where((panel_lane > panel_row) & (panel_lane < 8 * last), 0.0, panel)
                update = dot_over(panel, panel, 0, 0, highest)
                for r in range(last, n // 8):
                    mat[r] = jnp.where(inblock, 0.0, mat[r]) - update[8 * r : 8 * r + 8, :]
    full_row = lax.broadcasted_iota(jnp.int32, (n, n), 0)
    full_col = lax.broadcasted_iota(jnp.int32, (n, n), 1)
    return [jnp.where(full_col <= full_row, jnp.concatenate(mat, axis=0), 0.0) for mat in rows]


def three_pass(left, right, right_dim):
    (left_high, left_low), (right_high, right_low) = left, right
    return (
        dot_over(left_high, right_high, 1, right_dim)
        + dot_over(left_high, right_low, 1, right_dim)
        + dot_over(left_low, right_high, 1, right_dim)
    )


def right_kernel(
    slot, row_ref, right_ref, right_ops_ref, high_ref, low_ref, local_ref, right_mix, gated, right, sem
):
    states = right.shape[0]
    terms = gated.shape[0] // states
    wide = SITE * SITE
    local_cols = local_ref.shape[1]
    fetch = pltpu.make_async_copy(right_ref.at[slot], right, sem)
    fetch.start()
    spread = as_weights(one_hot((terms * wide, terms * SITE), lambda r: r // SITE, lambda c: c))
    widen = as_weights(one_hot((SITE, wide), lambda r: r, lambda c: c // SITE))
    same = one_hot((terms * wide, wide), lambda r: r % SITE, lambda c: c % SITE)
    for part, piece in enumerate(two_parts(right_ops_ref[...])):
        tall = dot_over(spread, piece, 1, 0).astype(jnp.bfloat16)
        full = dot_over(tall, widen, 1, 0)
        right_mix[:, part * wide : (part + 1) * wide] = jnp.where(same, full, 0.0).astype(
            jnp.bfloat16
        )
    fetch.wait()
    for pair in range(states // (2 * SITE)):
        base = pair * 2 * SITE
        halves = [
            jnp.concatenate(
                [
                    right[base + h * SITE : base + (h + 1) * SITE, j * states : (j + 1) * states]
                    for j in range(SITE)
                ],
                axis=0,
            )
            for h in range(2)
        ]
        block = jnp.concatenate(halves, axis=1)
        block = jnp.concatenate([block, block], axis=0)
        for t in range(terms):
            mixed = dot_over(right_mix[t * wide : (t + 1) * wide, :], block, 1, 0)
            mixed = mixed.astype(jnp.bfloat16)
            for h in range(2):
                for i in range(SITE):
                    gated[
                        t * states + base + h * SITE : t * states + base + (h + 1) * SITE,
                        i * states : (i + 1) * states,
                    ] = mixed[i * SITE : (i + 1) * SITE, h * states : (h + 1) * states]
    high_ref[...], low_ref[...] = two_parts(dot_over(gated[...], gated[...], 1, 1))
    offset = pl.multiple_of(row_ref[0] * local_cols, local_cols)
    local_ref[...] = gated[:, pl.ds(offset, local_cols)]


def gate_chunk(left_ref, slot, live, first_row, left_mix_ref, out_ref, out_first):
    chunk_rows, states = left_ref.shape[1:]
    terms, _, wide = left_mix_ref.shape
    turned = left_ref[slot].T
    pieces = []
    for b in range(chunk_rows // wide):
        lane = lax.broadcasted_iota(jnp.int32, (states, wide), 1)
        alive = lane < live * SITE - (first_row + b * wide)
        piece = turned[:, b * wide : (b + 1) * wide].astype(jnp.float32)
        pieces.append(jnp.where(alive, piece, 0.0).astype(jnp.bfloat16))
    tall = jnp.concatenate(pieces, axis=0)
    tall = jnp.concatenate([tall, tall], axis=1)
    for t in range(terms):
        mixed = dot_over(tall, left_mix_ref[t], 1, 0).astype(jnp.bfloat16)
        for b in range(len(pieces)):
            out_ref[
                slot, t * states : (t + 1) * states, out_first + b * wide : out_first + (b + 1) * wide
            ] = mixed[b * states : (b + 1) * states, :]


def own_kernel(row_ref, live_ref, left_ref, left_ops_ref, gated_ref, gram_ref, left_mix_ref):
    terms = left_ops_ref.shape[0]
    wide = SITE * SITE
    tall_pick = as_weights(one_hot((wide, SITE), lambda r: r % SITE, lambda c: c))
    wide_pick = as_weights(one_hot((SITE, wide), lambda r: r, lambda c: c % SITE))
    group = one_hot((wide, wide), lambda r: r // SITE, lambda c: c // SITE)
    for t in range(terms):
        for part, piece in enumerate(two_parts(left_ops_ref[t])):
            tall = dot_over(tall_pick, piece, 1, 1).astype(jnp.bfloat16)
            full = dot_over(tall, wide_pick, 1, 0)
            left_mix_ref[t, part * wide : (part + 1) * wide, :] = jnp.where(
                group, full, 0.0
            ).astype(jnp.bfloat16)
    slots, chunk_rows = left_ref.shape[:2]
    for s in range(slots):
        gate_chunk(left_ref, s, live_ref[s], row_ref[0] * chunk_rows, left_mix_ref, gated_ref, 0)
        gram_ref[s] = dot_over(gated_ref[s], gated_ref[s], 1, 1)


def krylov_kernel(row_ref, live_ref, kept_ref, weight_ref, *refs):
    chunks = len(refs) - 15
    left_refs = refs[:chunks]
    (left_mix_ref, own_ref, own_gram_ref, start_ref) = refs[chunks : chunks + 4]
    square_refs = refs[chunks + 4 : chunks + 8]
    (basis_ref, image_ref) = refs[chunks + 8 : chunks + 10]
    (gated, gram_high, gram_low, block, final) = refs[chunks + 10 :]
    slots, chunk_rows, states = left_refs[0].shape
    bond = own_ref.shape[1]
    keep = block.shape[1]
    for s in range(slots):
        for c in range(chunks):
            first_row = lax.rem(row_ref[0] + (chunks - c), chunks + 1) * chunk_rows
            gate_chunk(left_refs[c], s, live_ref[s], first_row, left_mix_ref, gated, c * chunk_rows)
        gram = own_gram_ref[s] + dot_over(gated[s], gated[s], 1, 1)
        gram_high[s], gram_low[s] = two_parts(gram)
        spots = lax.broadcasted_iota(jnp.int32, (keep, bond), 1)
        block[s] = jnp.where(spots == start_ref[s], 1.0, 0.0)

    def step(index, carry):
        images = [
            three_pass(two_parts(block[s]), (gram_high[s], gram_low[s]), 0) for s in range(slots)
        ]
        grams = [dot_over(images[s], block[s], 1, 1, highest) for s in range(slots)]
        inverses = lower_inverse(grams, WINDOW)
        for s in range(slots):
            image_ref[s] = three_pass(two_parts(inverses[s]), two_parts(images[s]), 0)

        @pl.when(index == ITERS)
        def _():
            for s in range(slots):
                final[s] = three_pass(two_parts(inverses[s]), two_parts(block[s]), 0)

        @pl.when(index < ITERS)
        def _():
            for s in range(slots):
                squares = (square_refs[2 * s][...], square_refs[2 * s + 1][...])
                scale = weight_ref[s] * weight_ref[s]
                block[s] = scale * three_pass(two_parts(image_ref[s]), squares, 0)

        return carry

    lax.fori_loop(0, ITERS + 1, step, 0)
    for s in range(slots):
        high, low = two_parts(final[s])
        basis = dot_over(high, own_ref[s], 1, 0) + dot_over(low, own_ref[s], 1, 0)
        keeps = lax.broadcasted_iota(jnp.int32, basis.shape, 0) < kept_ref[s]
        basis_ref[s] = jnp.where(keeps, basis, 0.0).T.astype(jnp.bfloat16)


def truncate_kernel(kept_ref, weight_ref, image_ref, *refs):
    square_refs, local_refs, (right_ref, total_ref) = refs[:4], refs[4:6], refs[6:]
    total = jnp.zeros((1, 1), jnp.float32)
    for s in range(image_ref.shape[0]):
        image = image_ref[s]
        high, low = two_parts(image)
        keeps = lax.broadcasted_iota(jnp.int32, image.shape, 0) < kept_ref[s]
        scale = weight_ref[s] * weight_ref[s]
        squares = (square_refs[2 * s][...], square_refs[2 * s + 1][...])
        squared = scale * three_pass((high, low), squares, 0) * image
        squared = jnp.where(keeps, squared, 0.0)
        total += jnp.sum(jnp.sum(squared, axis=0, keepdims=True), axis=1, keepdims=True)
        local = local_refs[s][...]
        part = dot_over(high, local, 1, 0) + dot_over(low, local, 1, 0)
        keeps = lax.broadcasted_iota(jnp.int32, part.shape, 0) < kept_ref[s]
        right_ref[s] = jnp.where(keeps, part * weight_ref[s], 0.0)
    total_ref[...] = jnp.broadcast_to(total, total_ref.shape)


def scale_kernel(totals_ref, part_ref, right_ref):
    total = jnp.sum(totals_ref[...], axis=0, keepdims=True)[:, :1]
    for s in range(part_ref.shape[0]):
        right_ref[s] = part_ref[s] * (1.0 / jnp.sqrt(total))


def smem():
    return pl.BlockSpec(memory_space=pltpu.SMEM)


def vmem():
    return pl.BlockSpec(memory_space=pltpu.VMEM)


def shape_of(shape, dtype):
    return jax.ShapeDtypeStruct(shape, dtype)


def kernel_options(mebibytes, flops):
    return dict(
        compiler_params=pltpu.CompilerParams(vmem_limit_bytes=mebibytes << 20),
        cost_estimate=pl.CostEstimate(flops=int(flops), bytes_accessed=2 << 20, transcendentals=0),
    )


def gate_right(slot, row, right_block, right_ops, local_cols):
    _, states, cols = right_block.shape
    terms = right_ops.shape[0]
    bond, wide = terms * states, SITE * SITE
    return pl.pallas_call(
        functools.partial(right_kernel, slot),
        in_specs=[smem(), pl.BlockSpec(memory_space=pltpu.HBM), vmem()],
        out_specs=[vmem()] * 3,
        out_shape=[
            shape_of((bond, bond), jnp.bfloat16),
            shape_of((bond, bond), jnp.bfloat16),
            shape_of((bond, local_cols), jnp.bfloat16),
        ],
        scratch_shapes=[
            pltpu.VMEM((terms * wide, 2 * wide), jnp.bfloat16),
            pltpu.VMEM((bond, cols), jnp.bfloat16),
            pltpu.VMEM((states, cols), jnp.bfloat16),
            pltpu.SemaphoreType.DMA,
        ],
        name="right_gate",
        **kernel_options(12, 4e9),
    )(row, right_block, right_ops.reshape(terms * SITE, SITE))


def gate_own(row, live, left, left_ops):
    slots, chunk_rows, states = left.shape
    terms = left_ops.shape[0]
    bond, wide = terms * states, SITE * SITE
    return pl.pallas_call(
        own_kernel,
        in_specs=[smem()] * 2 + [vmem()] * 2,
        out_specs=[vmem()] * 3,
        out_shape=[
            shape_of((slots, bond, chunk_rows), jnp.bfloat16),
            shape_of((slots, bond, bond), jnp.float32),
            shape_of((terms, 2 * wide, wide), jnp.bfloat16),
        ],
        name="own_gate",
        **kernel_options(8, 2e9),
    )(row, live, left, left_ops)


def krylov_part(row, live, kept, weight, left_chunks, left_mix, own, own_gram, start, squares):
    slots, chunk_rows, states = left_chunks[0].shape
    bond = own.shape[1]
    keep = start.shape[1]
    return pl.pallas_call(
        krylov_kernel,
        in_specs=[smem()] * 4 + [vmem()] * (len(left_chunks) + 4 + len(squares)),
        out_specs=[vmem()] * 2,
        out_shape=[
            shape_of((slots, chunk_rows, keep), jnp.bfloat16),
            shape_of((slots, keep, bond), jnp.float32),
        ],
        scratch_shapes=[
            pltpu.VMEM((slots, bond, len(left_chunks) * chunk_rows), jnp.bfloat16),
            pltpu.VMEM((slots, bond, bond), jnp.bfloat16),
            pltpu.VMEM((slots, bond, bond), jnp.bfloat16),
            pltpu.VMEM((slots, keep, bond), jnp.float32),
            pltpu.VMEM((slots, keep, bond), jnp.float32),
        ],
        name="krylov",
        **kernel_options(16, 2e10),
    )(row, live, kept, weight, *left_chunks, left_mix, own, own_gram, start, *squares)


def truncated(kept, weight, image, squares, locals_, peers):
    slots, keep, _ = image.shape
    local_cols = locals_[0].shape[1]
    return pl.pallas_call(
        truncate_kernel,
        in_specs=[smem()] * 2 + [vmem()] * (1 + len(squares) + len(locals_)),
        out_specs=[vmem()] * 2,
        out_shape=[
            shape_of((slots, keep, local_cols), jnp.float32),
            shape_of((peers, keep), jnp.float32),
        ],
        name="truncate",
        **kernel_options(8, 2e9),
    )(kept, weight, image, *squares, *locals_)


def scaled(totals, part):
    return pl.pallas_call(
        scale_kernel,
        in_specs=[vmem()] * 2,
        out_specs=vmem(),
        out_shape=shape_of(part.shape, jnp.float32),
        name="scale",
        **kernel_options(4, 1e6),
    )(totals, part)


def on_device(left_block, right_block, left_ops, right_ops, charges, live_states, kept, start):
    slots = left_block.shape[0]
    sectors = slots * lax.axis_size(SEC)
    top_bit = lax.axis_size(SEC).bit_length() - 2
    right_first = lax.axis_index(SEC) * slots
    left_first = (right_first + sectors // 2) % sectors
    cut = lambda table, first: lax.dynamic_slice_in_dim(table, first, slots, 0)
    row = lax.axis_index("row").astype(jnp.int32).reshape(1)
    live = cut(live_states, left_first)
    kept_here = cut(kept, right_first)
    weight = jnp.exp(-chemical * cut(charges, right_first).astype(jnp.float32))
    start_here = cut(start, left_first)[:, :, None]
    local_cols = right_block.shape[2] // lax.axis_size("row")
    left_theirs = from_partner(left_block, SEC, top_bit)
    first = list(gate_right(0, row, right_block, right_ops, local_cols))
    left_theirs, first[0], row_later = lax.optimization_barrier((left_theirs, first[0], row))
    rows = lax.axis_size("row")
    left_chunks = [
        lax.ppermute(left_theirs, "row", [(i, (i + d) % rows) for i in range(rows)])
        for d in range(1, rows)
    ]
    second = gate_right(1, row_later, right_block, right_ops, local_cols)
    own, own_gram, left_mix = gate_own(row_later, live, left_theirs, left_ops)
    squares = (*first[:2], *second[:2])
    basis, image = krylov_part(
        row, live, kept_here, weight, left_chunks, left_mix, own, own_gram, start_here, squares
    )
    basis = from_partner(basis, SEC, top_bit)
    right_part, total = truncated(
        kept_here, weight, image, squares, (first[2], second[2]), lax.axis_size(SEC)
    )
    totals = lax.all_to_all(total, SEC, split_axis=0, concat_axis=0, tiled=True)
    return basis.astype(jnp.float32), scaled(totals, right_part)


def solution(mesh):
    finer = Mesh(
        mesh.devices.reshape(8, 4, 2, mesh.shape["row"]), ("sec_0", "sec_1", "sec_2", "row")
    )
    in_specs = (P(SEC, "row", None), P(SEC, None, None), P(), P(), P(), P(), P(), P())
    out_specs = (P(SEC, "row", None), P(SEC, None, "row"))
    return jax.shard_map(
        on_device, mesh=finer, in_specs=in_specs, out_specs=out_specs, check_vma=False
    )
```

```python
import functools

import jax
import jax.numpy as jnp
from jax import lax
from jax.experimental import pallas as pl
from jax.experimental.pallas import tpu as pltpu
from jax.sharding import Mesh
from jax.sharding import PartitionSpec as P

SITE = 16
ITERS = 2
SEC = ("sec_0", "sec_1", "sec_2")
ROW = ("high", "low")
SEC_ROW = (*SEC, *ROW)
SEC_LOW = (*SEC, "low")
WINDOW = 64

chemical = 0.4
highest = lax.Precision.HIGHEST


def crossed(value, sec_mask, row_mask):
    rows = lax.axis_size(ROW)
    mask = sec_mask * rows + row_mask
    return lax.ppermute(value, SEC_ROW, [(i, i ^ mask) for i in range(lax.axis_size(SEC_ROW))])


def dot_over(left, right, left_dim, right_dim, precision=None):
    return lax.dot_general(
        left,
        right,
        (((left_dim,), (right_dim,)), ((), ())),
        precision=precision,
        preferred_element_type=jnp.float32,
    )


def two_parts(values):
    high = values.astype(jnp.bfloat16)
    low = (values - high.astype(jnp.float32)).astype(jnp.bfloat16)
    return high, low


def one_hot(shape, row_key, col_key):
    rows = lax.broadcasted_iota(jnp.int32, shape, 0)
    cols = lax.broadcasted_iota(jnp.int32, shape, 1)
    return row_key(rows) == col_key(cols)


def as_weights(mask):
    return jnp.where(mask, 1.0, 0.0).astype(jnp.bfloat16)


def lower_inverse(grams, window):
    n = grams[0].shape[0]
    lane = lax.broadcasted_iota(jnp.int32, (8, n), 1)
    sub = lax.broadcasted_iota(jnp.int32, (8, n), 0)
    rows = [[g[8 * q : 8 * q + 8, :] for q in range(n // 8)] for g in grams]
    span = window // 8
    for first in range(0, n // 8, span):
        last = first + span
        for q in range(first, last):
            k = 8 * q
            inside = (lane >= k) & (lane < k + 8)
            unit = (lane - k == sub).astype(jnp.float32)
            for mat in rows:
                cols = {
                    r: [jnp.broadcast_to(mat[r][:, k + m : k + m + 1], (8, n)) for m in range(8)]
                    for r in range(q, last)
                }
                for r in range(q, last):
                    mat[r] = jnp.where(inside, unit if r == q else 0.0, mat[r])
                pivot = jnp.broadcast_to(cols[q][0][0:1, :], (8, n))
                for m in range(8):
                    scale = lax.rsqrt(pivot)
                    weights = {
                        j: jnp.broadcast_to(cols[q][m][j : j + 1, :], (8, n)) * scale
                        for j in range(m + 1, 8)
                    }
                    if m < 7:
                        ahead = jnp.broadcast_to(cols[q][m + 1][m + 1 : m + 2, :], (8, n))
                        pivot = ahead - weights[m + 1] * weights[m + 1]
                    below = {r: cols[r][m] * scale for r in range(q, last)}
                    head = jnp.broadcast_to(mat[q][m : m + 1, :], (8, n)) * scale
                    for j in range(m + 1, 8):
                        for r in range(q, last):
                            cols[r][j] = cols[r][j] - below[r] * weights[j]
                    below[q] = jnp.where(sub > m, below[q], 0.0)
                    for r in range(q, last):
                        mat[r] = mat[r] - below[r] * head
                    mat[q] = jnp.where(sub == m, head, mat[q])
        if last < n // 8:
            inblock = (lane >= 8 * first) & (lane < 8 * last)
            for mat in rows:
                panel = jnp.concatenate(mat[first:last], axis=0)
                panel_row = lax.broadcasted_iota(jnp.int32, panel.shape, 0) + 8 * first
                panel_lane = lax.broadcasted_iota(jnp.int32, panel.shape, 1)
                panel = jnp.where((panel_lane > panel_row) & (panel_lane < 8 * last), 0.0, panel)
                update = dot_over(panel, panel, 0, 0, highest)
                for r in range(last, n // 8):
                    mat[r] = jnp.where(inblock, 0.0, mat[r]) - update[8 * r : 8 * r + 8, :]
    full_row = lax.broadcasted_iota(jnp.int32, (n, n), 0)
    full_col = lax.broadcasted_iota(jnp.int32, (n, n), 1)
    return [jnp.where(full_col <= full_row, jnp.concatenate(mat, axis=0), 0.0) for mat in rows]


def three_pass(left, right, right_dim):
    (left_high, left_low), (right_high, right_low) = left, right
    return (
        dot_over(left_high, right_high, 1, right_dim)
        + dot_over(left_high, right_low, 1, right_dim)
        + dot_over(left_low, right_high, 1, right_dim)
    )


def right_kernel(
    row_ref, right_ref, right_ops_ref, high_ref, low_ref, local_ref, right_mix, gated, right, sem
):
    states = right.shape[0]
    terms = gated.shape[0] // states
    wide = SITE * SITE
    local_cols = local_ref.shape[1]
    fetch = pltpu.make_async_copy(right_ref.at[lax.rem(row_ref[0], 2)], right, sem)
    fetch.start()
    spread = as_weights(one_hot((terms * wide, terms * SITE), lambda r: r // SITE, lambda c: c))
    widen = as_weights(one_hot((SITE, wide), lambda r: r, lambda c: c // SITE))
    same = one_hot((terms * wide, wide), lambda r: r % SITE, lambda c: c % SITE)
    for part, piece in enumerate(two_parts(right_ops_ref[...])):
        tall = dot_over(spread, piece, 1, 0).astype(jnp.bfloat16)
        full = dot_over(tall, widen, 1, 0)
        right_mix[:, part * wide : (part + 1) * wide] = jnp.where(same, full, 0.0).astype(
            jnp.bfloat16
        )
    fetch.wait()
    for pair in range(states // (2 * SITE)):
        base = pair * 2 * SITE
        halves = [
            jnp.concatenate(
                [
                    right[base + h * SITE : base + (h + 1) * SITE, j * states : (j + 1) * states]
                    for j in range(SITE)
                ],
                axis=0,
            )
            for h in range(2)
        ]
        block = jnp.concatenate(halves, axis=1)
        block = jnp.concatenate([block, block], axis=0)
        for t in range(terms):
            mixed = dot_over(right_mix[t * wide : (t + 1) * wide, :], block, 1, 0)
            mixed = mixed.astype(jnp.bfloat16)
            for h in range(2):
                for i in range(SITE):
                    gated[
                        t * states + base + h * SITE : t * states + base + (h + 1) * SITE,
                        i * states : (i + 1) * states,
                    ] = mixed[i * SITE : (i + 1) * SITE, h * states : (h + 1) * states]
    high_ref[...], low_ref[...] = two_parts(dot_over(gated[...], gated[...], 1, 1))
    offset = pl.multiple_of((row_ref[0] // 2) * local_cols, local_cols)
    local_ref[...] = gated[:, pl.ds(offset, local_cols)]


def build_left_mix(left_ops_ref, left_mix):
    terms, _, wide = left_mix.shape
    tall_pick = as_weights(one_hot((wide, SITE), lambda r: r % SITE, lambda c: c))
    wide_pick = as_weights(one_hot((SITE, wide), lambda r: r, lambda c: c % SITE))
    group = one_hot((wide, wide), lambda r: r // SITE, lambda c: c // SITE)
    for t in range(terms):
        for part, piece in enumerate(two_parts(left_ops_ref[t])):
            tall = dot_over(tall_pick, piece, 1, 1).astype(jnp.bfloat16)
            full = dot_over(tall, wide_pick, 1, 0)
            left_mix[t, part * wide : (part + 1) * wide, :] = jnp.where(
                group, full, 0.0
            ).astype(jnp.bfloat16)


def gate_chunk(left_ref, live, first_row, left_mix_ref, gated, out_first):
    chunk_rows, states = left_ref.shape
    terms, _, wide = left_mix_ref.shape
    turned = left_ref[...].T
    pieces = []
    for b in range(chunk_rows // wide):
        lane = lax.broadcasted_iota(jnp.int32, (states, wide), 1)
        alive = lane < live * SITE - (first_row + b * wide)
        piece = turned[:, b * wide : (b + 1) * wide].astype(jnp.float32)
        pieces.append(jnp.where(alive, piece, 0.0).astype(jnp.bfloat16))
    tall = jnp.concatenate(pieces, axis=0)
    tall = jnp.concatenate([tall, tall], axis=1)
    for t in range(terms):
        mixed = dot_over(tall, left_mix_ref[t], 1, 0).astype(jnp.bfloat16)
        for b in range(len(pieces)):
            gated[
                t * states : (t + 1) * states, out_first + b * wide : out_first + (b + 1) * wide
            ] = mixed[b * states : (b + 1) * states, :]


def krylov_kernel(row_ref, live_ref, kept_ref, weight_ref, *refs):
    chunks = len(refs) - 13
    left_refs = refs[:chunks]
    (left_ops_ref, start_ref, square_high, square_low) = refs[chunks : chunks + 4]
    (own_ref, other_ref, image_ref) = refs[chunks + 4 : chunks + 7]
    (gated, gram_high, gram_low, block, final, left_mix) = refs[chunks + 7 :]
    build_left_mix(left_ops_ref, left_mix)
    chunk_rows = left_refs[0].shape[0]
    bond, keep = image_ref.shape[1], image_ref.shape[0]
    for c in range(chunks):
        first_row = lax.bitwise_xor(row_ref[0], c) * chunk_rows
        gate_chunk(left_refs[c], live_ref[0], first_row, left_mix, gated, c * chunk_rows)
    gram_high[...], gram_low[...] = two_parts(dot_over(gated[...], gated[...], 1, 1))
    spots = lax.broadcasted_iota(jnp.int32, (keep, bond), 1)
    block[...] = jnp.where(spots == start_ref[...], 1.0, 0.0)

    def step(index, carry):
        images = three_pass(two_parts(block[...]), (gram_high[...], gram_low[...]), 0)
        (inverse,) = lower_inverse([dot_over(images, block[...], 1, 1, highest)], WINDOW)
        inverse = two_parts(inverse)
        image_ref[...] = three_pass(inverse, two_parts(images), 0)

        @pl.when(index == ITERS)
        def _():
            final[...] = three_pass(inverse, two_parts(block[...]), 0)

        @pl.when(index < ITERS)
        def _():
            squares = (square_high[...], square_low[...])
            scale = weight_ref[0] * weight_ref[0]
            block[...] = scale * three_pass(two_parts(image_ref[...]), squares, 0)

        return carry

    lax.fori_loop(0, ITERS + 1, step, 0)
    high, low = two_parts(final[...])
    for c, basis_ref in enumerate((own_ref, other_ref)):
        rows = gated[:, c * chunk_rows : (c + 1) * chunk_rows]
        basis = dot_over(high, rows, 1, 0) + dot_over(low, rows, 1, 0)
        keeps = lax.broadcasted_iota(jnp.int32, basis.shape, 0) < kept_ref[0]
        basis_ref[...] = jnp.where(keeps, basis, 0.0).T.astype(jnp.bfloat16)


def truncate_kernel(
    row_ref, kept_ref, weight_ref, image_ref, square_high, square_low, local_ref,
    own_ref, other_ref, total_ref,
):
    image = image_ref[...]
    high, low = two_parts(image)
    keeps = lax.broadcasted_iota(jnp.int32, image.shape, 0) < kept_ref[0]
    scale = weight_ref[0] * weight_ref[0]
    squared = scale * three_pass((high, low), (square_high[...], square_low[...]), 0) * image
    squared = jnp.where(keeps, squared, 0.0)
    total = jnp.sum(jnp.sum(squared, axis=0, keepdims=True), axis=1, keepdims=True)
    total_ref[...] = jnp.broadcast_to(total, total_ref.shape)
    cols = own_ref.shape[1]
    side = lax.rem(row_ref[0], 2)
    for out_ref, half in ((own_ref, side), (other_ref, 1 - side)):
        local = local_ref[:, pl.ds(pl.multiple_of(half * cols, cols), cols)]
        part = dot_over(high, local, 1, 0) + dot_over(low, local, 1, 0)
        keeps = lax.broadcasted_iota(jnp.int32, part.shape, 0) < kept_ref[0]
        out_ref[...] = jnp.where(keeps, part * weight_ref[0], 0.0).astype(out_ref.dtype)


def finish_kernel(
    row_ref, totals_ref, part_own, part_other, basis_own, basis_other, basis_ref, right_ref
):
    side = lax.rem(row_ref[0], 2)
    basis_ref[side] = basis_own[...].astype(jnp.float32)
    basis_ref[1 - side] = basis_other[...].astype(jnp.float32)
    total = jnp.sum(totals_ref[...], axis=0, keepdims=True)[:, :1]
    factor = 1.0 / jnp.sqrt(total)
    right_ref[side] = part_own[...] * factor
    right_ref[1 - side] = part_other[...].astype(jnp.float32) * factor


def smem():
    return pl.BlockSpec(memory_space=pltpu.SMEM)


def vmem():
    return pl.BlockSpec(memory_space=pltpu.VMEM)


def shape_of(shape, dtype):
    return jax.ShapeDtypeStruct(shape, dtype)


def kernel_options(mebibytes, flops):
    return dict(
        compiler_params=pltpu.CompilerParams(vmem_limit_bytes=mebibytes << 20),
        cost_estimate=pl.CostEstimate(flops=int(flops), bytes_accessed=2 << 20, transcendentals=0),
    )


def gate_right(row, right_block, right_ops, local_cols):
    _, states, cols = right_block.shape
    terms = right_ops.shape[0]
    bond, wide = terms * states, SITE * SITE
    return pl.pallas_call(
        right_kernel,
        in_specs=[smem(), pl.BlockSpec(memory_space=pltpu.HBM), vmem()],
        out_specs=[vmem()] * 3,
        out_shape=[
            shape_of((bond, bond), jnp.bfloat16),
            shape_of((bond, bond), jnp.bfloat16),
            shape_of((bond, local_cols), jnp.bfloat16),
        ],
        scratch_shapes=[
            pltpu.VMEM((terms * wide, 2 * wide), jnp.bfloat16),
            pltpu.VMEM((bond, cols), jnp.bfloat16),
            pltpu.VMEM((states, cols), jnp.bfloat16),
            pltpu.SemaphoreType.DMA,
        ],
        name="right_gate",
        **kernel_options(12, 4e9),
    )(row, right_block, right_ops.reshape(terms * SITE, SITE))


def krylov_part(row, live, kept, weight, left_chunks, left_ops, start, squares):
    chunk_rows, _ = left_chunks[0].shape
    bond = squares[0].shape[0]
    keep = start.shape[0]
    return pl.pallas_call(
        krylov_kernel,
        in_specs=[smem()] * 4 + [vmem()] * (len(left_chunks) + 4),
        out_specs=[vmem()] * 3,
        out_shape=[
            shape_of((chunk_rows, keep), jnp.bfloat16),
            shape_of((chunk_rows, keep), jnp.bfloat16),
            shape_of((keep, bond), jnp.float32),
        ],
        scratch_shapes=[
            pltpu.VMEM((bond, len(left_chunks) * chunk_rows), jnp.bfloat16),
            pltpu.VMEM((bond, bond), jnp.bfloat16),
            pltpu.VMEM((bond, bond), jnp.bfloat16),
            pltpu.VMEM((keep, bond), jnp.float32),
            pltpu.VMEM((keep, bond), jnp.float32),
            pltpu.VMEM((left_ops.shape[0], 2 * SITE * SITE, SITE * SITE), jnp.bfloat16),
        ],
        name="krylov",
        **kernel_options(14, 2e10),
    )(row, live, kept, weight, *left_chunks, left_ops, start, *squares)


def truncated(row, kept, weight, image, squares, local, peers):
    keep, _ = image.shape
    cols = local.shape[1] // 2
    return pl.pallas_call(
        truncate_kernel,
        in_specs=[smem()] * 3 + [vmem()] * 4,
        out_specs=[vmem()] * 3,
        out_shape=[
            shape_of((keep, cols), jnp.float32),
            shape_of((keep, cols), jnp.bfloat16),
            shape_of((peers, keep), jnp.float32),
        ],
        name="truncate",
        **kernel_options(8, 2e9),
    )(row, kept, weight, image, *squares, local)


def finished(row, totals, part_own, part_other, basis_own, basis_other):
    keep, cols = part_own.shape
    return pl.pallas_call(
        finish_kernel,
        in_specs=[smem()] + [vmem()] * 5,
        out_specs=[vmem()] * 2,
        out_shape=[
            shape_of((2, *basis_own.shape), jnp.float32),
            shape_of((2, keep, cols), jnp.float32),
        ],
        name="finish",
        **kernel_options(4, 1e6),
    )(row, totals, part_own, part_other, basis_own, basis_other)


def on_device(left_block, right_block, left_ops, right_ops, charges, live_states, kept, start):
    slots = left_block.shape[0]
    sec_size, row_size = lax.axis_size(SEC), lax.axis_size(ROW)
    sectors = slots * sec_size
    sec_half = sec_size // 2
    side = lax.axis_index("low")
    row = lax.axis_index(ROW).astype(jnp.int32).reshape(1)
    mine = jnp.where(side == 0, left_block[0], left_block[1])
    neighbours = jnp.where(side == 0, left_block[1], left_block[0])
    left_chunks = [crossed((mine, neighbours)[d % 2], sec_half, d) for d in range(row_size)]
    right_id = lax.axis_index(SEC) * slots + side
    left_id = (right_id + sectors // 2) % sectors
    cut = lambda table, which: lax.dynamic_slice_in_dim(table, which, 1, 0)
    live = cut(live_states, left_id)
    kept_here = cut(kept, right_id)
    weight = jnp.exp(-chemical * cut(charges, right_id).astype(jnp.float32))
    start_here = cut(start, left_id).reshape(-1, 1)
    local_cols = 2 * right_block.shape[2] // row_size
    high, low, local = gate_right(row, right_block, right_ops, local_cols)
    basis_own, basis_other, image = krylov_part(
        row, live, kept_here, weight, left_chunks, left_ops, start_here, (high, low)
    )
    basis_own = crossed(basis_own, sec_half, 0)
    basis_other = crossed(basis_other, sec_half, 1)
    part_own, part_other, total = truncated(
        row, kept_here, weight, image, (high, low), local, lax.axis_size(SEC_LOW)
    )
    part_other = crossed(part_other, 0, 1)
    totals = lax.all_to_all(total, SEC_LOW, split_axis=0, concat_axis=0, tiled=True)
    return tuple(finished(row, totals, part_own, part_other, basis_own, basis_other))


def solution(mesh):
    finer = Mesh(mesh.devices.reshape(8, 4, 2, 2, 2), SEC_ROW)
    in_specs = (P(SEC, ROW, None), P(SEC, None, None), P(), P(), P(), P(), P(), P())
    out_specs = (P(SEC, ROW, None), P(SEC, None, ROW))
    return jax.shard_map(
        on_device, mesh=finer, in_specs=in_specs, out_specs=out_specs, check_vma=False
    )
```

```python
import functools

import jax
import jax.numpy as jnp
from jax import lax
from jax.experimental import pallas as pl
from jax.experimental.pallas import tpu as pltpu
from jax.sharding import Mesh
from jax.sharding import PartitionSpec as P

SITE = 16
ITERS = 2
SEC = ("sec_0", "sec_1", "sec_2")
SEC_ROW = ("sec_0", "sec_1", "sec_2", "row")
WINDOW = 32

chemical = 0.4
highest = lax.Precision.HIGHEST


def from_partner(value, axis, distance):
    mask = 2**distance
    pairs = [(source, source ^ mask) for source in range(lax.axis_size(axis))]
    return lax.ppermute(value, axis, pairs)


def dot_over(left, right, left_dim, right_dim, precision=None):
    return lax.dot_general(
        left,
        right,
        (((left_dim,), (right_dim,)), ((), ())),
        precision=precision,
        preferred_element_type=jnp.float32,
    )


def two_parts(values):
    high = values.astype(jnp.bfloat16)
    low = (values - high.astype(jnp.float32)).astype(jnp.bfloat16)
    return high, low


def one_hot(shape, row_key, col_key):
    rows = lax.broadcasted_iota(jnp.int32, shape, 0)
    cols = lax.broadcasted_iota(jnp.int32, shape, 1)
    return row_key(rows) == col_key(cols)


def as_weights(mask):
    return jnp.where(mask, 1.0, 0.0).astype(jnp.bfloat16)


def lower_inverse(grams, window):
    n = grams[0].shape[0]
    lane = lax.broadcasted_iota(jnp.int32, (8, n), 1)
    sub = lax.broadcasted_iota(jnp.int32, (8, n), 0)
    rows = [[g[8 * q : 8 * q + 8, :] for q in range(n // 8)] for g in grams]
    span = window // 8
    for first in range(0, n // 8, span):
        last = first + span
        for q in range(first, last):
            k = 8 * q
            inside = (lane >= k) & (lane < k + 8)
            unit = (lane - k == sub).astype(jnp.float32)
            for mat in rows:
                cols = {
                    r: [jnp.broadcast_to(mat[r][:, k + m : k + m + 1], (8, n)) for m in range(8)]
                    for r in range(q, last)
                }
                for r in range(q, last):
                    mat[r] = jnp.where(inside, unit if r == q else 0.0, mat[r])
                pivot = jnp.broadcast_to(cols[q][0][0:1, :], (8, n))
                for m in range(8):
                    scale = lax.rsqrt(pivot)
                    weights = {
                        j: jnp.broadcast_to(cols[q][m][j : j + 1, :], (8, n)) * scale
                        for j in range(m + 1, 8)
                    }
                    if m < 7:
                        ahead = jnp.broadcast_to(cols[q][m + 1][m + 1 : m + 2, :], (8, n))
                        pivot = ahead - weights[m + 1] * weights[m + 1]
                    below = {r: cols[r][m] * scale for r in range(q, last)}
                    head = jnp.broadcast_to(mat[q][m : m + 1, :], (8, n)) * scale
                    for j in range(m + 1, 8):
                        for r in range(q, last):
                            cols[r][j] = cols[r][j] - below[r] * weights[j]
                    below[q] = jnp.where(sub > m, below[q], 0.0)
                    for r in range(q, last):
                        mat[r] = mat[r] - below[r] * head
                    mat[q] = jnp.where(sub == m, head, mat[q])
        if last < n // 8:
            inblock = (lane >= 8 * first) & (lane < 8 * last)
            for mat in rows:
                panel = jnp.concatenate(mat[first:last], axis=0)
                panel_row = lax.broadcasted_iota(jnp.int32, panel.shape, 0) + 8 * first
                panel_lane = lax.broadcasted_iota(jnp.int32, panel.shape, 1)
                panel = jnp.where((panel_lane > panel_row) & (panel_lane < 8 * last), 0.0, panel)
                update = dot_over(panel, panel, 0, 0, highest)
                for r in range(last, n // 8):
                    mat[r] = jnp.where(inblock, 0.0, mat[r]) - update[8 * r : 8 * r + 8, :]
    full_row = lax.broadcasted_iota(jnp.int32, (n, n), 0)
    full_col = lax.broadcasted_iota(jnp.int32, (n, n), 1)
    return [jnp.where(full_col <= full_row, jnp.concatenate(mat, axis=0), 0.0) for mat in rows]


def three_pass(left, right, right_dim):
    (left_high, left_low), (right_high, right_low) = left, right
    return (
        dot_over(left_high, right_high, 1, right_dim)
        + dot_over(left_high, right_low, 1, right_dim)
        + dot_over(left_low, right_high, 1, right_dim)
    )


def right_kernel(
    slot, row_ref, right_ref, right_ops_ref, high_ref, low_ref, local_ref, right_mix, gated, right, sem
):
    states = right.shape[0]
    terms = gated.shape[0] // states
    wide = SITE * SITE
    local_cols = local_ref.shape[1]
    fetch = pltpu.make_async_copy(right_ref.at[slot], right, sem)
    fetch.start()
    spread = as_weights(one_hot((terms * wide, terms * SITE), lambda r: r // SITE, lambda c: c))
    widen = as_weights(one_hot((SITE, wide), lambda r: r, lambda c: c // SITE))
    same = one_hot((terms * wide, wide), lambda r: r % SITE, lambda c: c % SITE)
    for part, piece in enumerate(two_parts(right_ops_ref[...])):
        tall = dot_over(spread, piece, 1, 0).astype(jnp.bfloat16)
        full = dot_over(tall, widen, 1, 0)
        right_mix[:, part * wide : (part + 1) * wide] = jnp.where(same, full, 0.0).astype(
            jnp.bfloat16
        )
    fetch.wait()
    for pair in range(states // (2 * SITE)):
        base = pair * 2 * SITE
        halves = [
            jnp.concatenate(
                [
                    right[base + h * SITE : base + (h + 1) * SITE, j * states : (j + 1) * states]
                    for j in range(SITE)
                ],
                axis=0,
            )
            for h in range(2)
        ]
        block = jnp.concatenate(halves, axis=1)
        block = jnp.concatenate([block, block], axis=0)
        for t in range(terms):
            mixed = dot_over(right_mix[t * wide : (t + 1) * wide, :], block, 1, 0)
            mixed = mixed.astype(jnp.bfloat16)
            for h in range(2):
                for i in range(SITE):
                    gated[
                        t * states + base + h * SITE : t * states + base + (h + 1) * SITE,
                        i * states : (i + 1) * states,
                    ] = mixed[i * SITE : (i + 1) * SITE, h * states : (h + 1) * states]
    high_ref[...], low_ref[...] = two_parts(dot_over(gated[...], gated[...], 1, 1))
    offset = pl.multiple_of(row_ref[0] * local_cols, local_cols)
    local_ref[...] = gated[:, pl.ds(offset, local_cols)]


def build_left_mix(left_ops_ref, left_mix):
    terms, _, wide = left_mix.shape
    tall_pick = as_weights(one_hot((wide, SITE), lambda r: r % SITE, lambda c: c))
    wide_pick = as_weights(one_hot((SITE, wide), lambda r: r, lambda c: c % SITE))
    group = one_hot((wide, wide), lambda r: r // SITE, lambda c: c // SITE)
    for t in range(terms):
        for part, piece in enumerate(two_parts(left_ops_ref[t])):
            tall = dot_over(tall_pick, piece, 1, 1).astype(jnp.bfloat16)
            full = dot_over(tall, wide_pick, 1, 0)
            left_mix[t, part * wide : (part + 1) * wide, :] = jnp.where(group, full, 0.0).astype(
                jnp.bfloat16
            )


def gate_chunk(left_ref, live, first_row, left_mix_ref, gated, out_first):
    chunk_rows, states = left_ref.shape
    terms, _, wide = left_mix_ref.shape
    turned = left_ref[...].T
    pieces = []
    for b in range(chunk_rows // wide):
        lane = lax.broadcasted_iota(jnp.int32, (states, wide), 1)
        alive = lane < live * SITE - (first_row + b * wide)
        piece = turned[:, b * wide : (b + 1) * wide].astype(jnp.float32)
        pieces.append(jnp.where(alive, piece, 0.0).astype(jnp.bfloat16))
    tall = jnp.concatenate(pieces, axis=0)
    tall = jnp.concatenate([tall, tall], axis=1)
    for t in range(terms):
        mixed = dot_over(tall, left_mix_ref[t], 1, 0).astype(jnp.bfloat16)
        for b in range(len(pieces)):
            gated[
                t * states : (t + 1) * states, out_first + b * wide : out_first + (b + 1) * wide
            ] = mixed[b * states : (b + 1) * states, :]


def gate_sector(row_ref, live, left_refs, left_mix, gated):
    chunks = len(left_refs)
    chunk_rows = left_refs[0].shape[0]
    for c in range(chunks):
        first_row = lax.rem(row_ref[0] + (chunks - c), chunks) * chunk_rows
        gate_chunk(left_refs[c], live, first_row, left_mix, gated, c * chunk_rows)
    return two_parts(dot_over(gated[...], gated[...], 1, 1))


def left_kernel(row_ref, live_ref, left_ops_ref, *refs):
    left_refs = refs[:-5]
    own_ref, high_ref, low_ref, left_mix, gated = refs[-5:]
    build_left_mix(left_ops_ref, left_mix)
    high_ref[...], low_ref[...] = gate_sector(row_ref, live_ref[0], left_refs, left_mix, gated)
    own_ref[...] = gated[:, : own_ref.shape[1]]


def krylov_kernel(row_ref, live_ref, kept_ref, weight_ref, *refs):
    chunks = len(refs) - 16
    left_refs = refs[:chunks]
    (left_mix, first_own, first_high, first_low, start_ref) = refs[chunks : chunks + 5]
    square_refs = refs[chunks + 5 : chunks + 9]
    (basis_ref, image_ref) = refs[chunks + 9 : chunks + 11]
    (gated, second_high, second_low, block, final) = refs[chunks + 11 :]
    slots, keep, bond = image_ref.shape
    chunk_rows = left_refs[0].shape[0]
    second_high[...], second_low[...] = gate_sector(row_ref, live_ref[1], left_refs, left_mix, gated)
    gram_refs = ((first_high, first_low), (second_high, second_low))
    for s in range(slots):
        spots = lax.broadcasted_iota(jnp.int32, (keep, bond), 1)
        block[s] = jnp.where(spots == start_ref[s], 1.0, 0.0)

    def step(index, carry):
        images = [
            three_pass(two_parts(block[s]), (gram_refs[s][0][...], gram_refs[s][1][...]), 0)
            for s in range(slots)
        ]
        grams = [dot_over(images[s], block[s], 1, 1, highest) for s in range(slots)]
        inverses = [two_parts(inverse) for inverse in lower_inverse(grams, WINDOW)]
        for s in range(slots):
            image_ref[s] = three_pass(inverses[s], two_parts(images[s]), 0)

        @pl.when(index == ITERS)
        def _():
            for s in range(slots):
                final[s] = three_pass(inverses[s], two_parts(block[s]), 0)

        @pl.when(index < ITERS)
        def _():
            for s in range(slots):
                squares = (square_refs[2 * s][...], square_refs[2 * s + 1][...])
                scale = weight_ref[s] * weight_ref[s]
                block[s] = scale * three_pass(two_parts(image_ref[s]), squares, 0)

        return carry

    lax.fori_loop(0, ITERS + 1, step, 0)
    for s, rows in enumerate((first_own[...], gated[:, :chunk_rows])):
        high, low = two_parts(final[s])
        basis = dot_over(high, rows, 1, 0) + dot_over(low, rows, 1, 0)
        keeps = lax.broadcasted_iota(jnp.int32, basis.shape, 0) < kept_ref[s]
        basis_ref[s] = jnp.where(keeps, basis, 0.0).T.astype(jnp.bfloat16)


def truncate_kernel(kept_ref, weight_ref, image_ref, *refs):
    square_refs, local_refs, (right_ref, total_ref) = refs[:4], refs[4:6], refs[6:]
    total = jnp.zeros((1, 1), jnp.float32)
    for s in range(image_ref.shape[0]):
        image = image_ref[s]
        high, low = two_parts(image)
        keeps = lax.broadcasted_iota(jnp.int32, image.shape, 0) < kept_ref[s]
        scale = weight_ref[s] * weight_ref[s]
        squares = (square_refs[2 * s][...], square_refs[2 * s + 1][...])
        squared = scale * three_pass((high, low), squares, 0) * image
        squared = jnp.where(keeps, squared, 0.0)
        total += jnp.sum(jnp.sum(squared, axis=0, keepdims=True), axis=1, keepdims=True)
        local = local_refs[s][...]
        part = dot_over(high, local, 1, 0) + dot_over(low, local, 1, 0)
        keeps = lax.broadcasted_iota(jnp.int32, part.shape, 0) < kept_ref[s]
        right_ref[s] = jnp.where(keeps, part * weight_ref[s], 0.0)
    total_ref[...] = jnp.broadcast_to(total, total_ref.shape)


def finish_kernel(totals_ref, part_ref, sent_ref, basis_ref, right_ref):
    basis_ref[...] = sent_ref[...].astype(jnp.float32)
    total = jnp.sum(totals_ref[...], axis=0, keepdims=True)[:, :1]
    factor = 1.0 / jnp.sqrt(total)
    for s in range(part_ref.shape[0]):
        right_ref[s] = part_ref[s] * factor


def smem():
    return pl.BlockSpec(memory_space=pltpu.SMEM)


def vmem():
    return pl.BlockSpec(memory_space=pltpu.VMEM)


def shape_of(shape, dtype):
    return jax.ShapeDtypeStruct(shape, dtype)


def kernel_options(mebibytes, flops):
    return dict(
        compiler_params=pltpu.CompilerParams(vmem_limit_bytes=mebibytes << 20),
        cost_estimate=pl.CostEstimate(flops=int(flops), bytes_accessed=2 << 20, transcendentals=0),
    )


def gate_right(slot, row, right_block, right_ops, local_cols):
    _, states, cols = right_block.shape
    terms = right_ops.shape[0]
    bond, wide = terms * states, SITE * SITE
    return pl.pallas_call(
        functools.partial(right_kernel, slot),
        in_specs=[smem(), pl.BlockSpec(memory_space=pltpu.HBM), vmem()],
        out_specs=[vmem()] * 3,
        out_shape=[
            shape_of((bond, bond), jnp.bfloat16),
            shape_of((bond, bond), jnp.bfloat16),
            shape_of((bond, local_cols), jnp.bfloat16),
        ],
        scratch_shapes=[
            pltpu.VMEM((terms * wide, 2 * wide), jnp.bfloat16),
            pltpu.VMEM((bond, cols), jnp.bfloat16),
            pltpu.VMEM((states, cols), jnp.bfloat16),
            pltpu.SemaphoreType.DMA,
        ],
        name="right_gate",
        **kernel_options(12, 4e9),
    )(row, right_block, right_ops.reshape(terms * SITE, SITE))


def gate_left(row, live, left_chunks, left_ops):
    chunk_rows, states = left_chunks[0].shape
    terms = left_ops.shape[0]
    bond, wide = terms * states, SITE * SITE
    return pl.pallas_call(
        left_kernel,
        in_specs=[smem()] * 2 + [vmem()] * (1 + len(left_chunks)),
        out_specs=[vmem()] * 4,
        out_shape=[
            shape_of((bond, chunk_rows), jnp.bfloat16),
            shape_of((bond, bond), jnp.bfloat16),
            shape_of((bond, bond), jnp.bfloat16),
            shape_of((terms, 2 * wide, wide), jnp.bfloat16),
        ],
        scratch_shapes=[pltpu.VMEM((bond, len(left_chunks) * chunk_rows), jnp.bfloat16)],
        name="left_gate",
        **kernel_options(10, 4e9),
    )(row, live, left_ops, *left_chunks)


def krylov_part(row, live, kept, weight, left_chunks, left_mix, first, start, squares):
    chunk_rows, _ = left_chunks[0].shape
    bond = squares[0].shape[0]
    slots, keep, _ = start.shape
    return pl.pallas_call(
        krylov_kernel,
        in_specs=[smem()] * 4 + [vmem()] * (len(left_chunks) + 2 + len(first) + len(squares)),
        out_specs=[vmem()] * 2,
        out_shape=[
            shape_of((slots, chunk_rows, keep), jnp.bfloat16),
            shape_of((slots, keep, bond), jnp.float32),
        ],
        scratch_shapes=[
            pltpu.VMEM((bond, len(left_chunks) * chunk_rows), jnp.bfloat16),
            pltpu.VMEM((bond, bond), jnp.bfloat16),
            pltpu.VMEM((bond, bond), jnp.bfloat16),
            pltpu.VMEM((slots, keep, bond), jnp.float32),
            pltpu.VMEM((slots, keep, bond), jnp.float32),
        ],
        name="krylov",
        **kernel_options(14, 2e10),
    )(row, live, kept, weight, *left_chunks, left_mix, *first, start, *squares)


def truncated(kept, weight, image, squares, locals_, peers):
    slots, keep, _ = image.shape
    local_cols = locals_[0].shape[1]
    return pl.pallas_call(
        truncate_kernel,
        in_specs=[smem()] * 2 + [vmem()] * (1 + len(squares) + len(locals_)),
        out_specs=[vmem()] * 2,
        out_shape=[
            shape_of((slots, keep, local_cols), jnp.float32),
            shape_of((peers, keep), jnp.float32),
        ],
        name="truncate",
        **kernel_options(8, 2e9),
    )(kept, weight, image, *squares, *locals_)


def finished(totals, part, sent):
    return pl.pallas_call(
        finish_kernel,
        in_specs=[vmem()] * 3,
        out_specs=[vmem()] * 2,
        out_shape=[shape_of(sent.shape, jnp.float32), shape_of(part.shape, jnp.float32)],
        name="finish",
        **kernel_options(4, 1e6),
    )(totals, part, sent)


def on_device(left_block, right_block, left_ops, right_ops, charges, live_states, kept, start):
    slots = left_block.shape[0]
    sectors = slots * lax.axis_size(SEC)
    top_bit = lax.axis_size(SEC).bit_length() - 2
    right_first = lax.axis_index(SEC) * slots
    left_first = (right_first + sectors // 2) % sectors
    cut = lambda table, first: lax.dynamic_slice_in_dim(table, first, slots, 0)
    row = lax.axis_index("row").astype(jnp.int32).reshape(1)
    live = cut(live_states, left_first)
    kept_here = cut(kept, right_first)
    weight = jnp.exp(-chemical * cut(charges, right_first).astype(jnp.float32))
    start_here = cut(start, left_first)[:, :, None]
    local_cols = right_block.shape[2] // lax.axis_size("row")
    rows = lax.axis_size("row")

    def over_rows(chunk):
        sent = [
            lax.ppermute(chunk, "row", [(i, (i + d) % rows) for i in range(rows)])
            for d in range(1, rows)
        ]
        return [chunk, *sent]

    theirs = [from_partner(left_block[s], SEC, top_bit) for s in range(slots)]
    first = list(gate_right(0, row, right_block, right_ops, local_cols))
    theirs[0], first[0], row_second = lax.optimization_barrier((theirs[0], first[0], row))
    first_chunks = over_rows(theirs[0])
    second = list(gate_right(1, row_second, right_block, right_ops, local_cols))
    theirs[1], second[0], row_left = lax.optimization_barrier((theirs[1], second[0], row))
    second_chunks = over_rows(theirs[1])
    *first_left, left_mix = gate_left(row_left, live, first_chunks, left_ops)
    squares = (*first[:2], *second[:2])
    basis, image = krylov_part(
        row, live, kept_here, weight, second_chunks, left_mix, first_left, start_here, squares
    )
    basis = from_partner(basis, SEC, top_bit)
    right_part, total = truncated(
        kept_here, weight, image, squares, (first[2], second[2]), lax.axis_size(SEC)
    )
    totals = lax.all_to_all(total, SEC, split_axis=0, concat_axis=0, tiled=True)
    return tuple(finished(totals, right_part, basis))


def solution(mesh):
    finer = Mesh(
        mesh.devices.reshape(8, 4, 2, mesh.shape["row"]), ("sec_0", "sec_1", "sec_2", "row")
    )
    in_specs = (P(SEC, "row", None), P(SEC, None, None), P(), P(), P(), P(), P(), P())
    out_specs = (P(SEC, "row", None), P(SEC, None, "row"))
    return jax.shard_map(
        on_device, mesh=finer, in_specs=in_specs, out_specs=out_specs, check_vma=False
    )
```

```python
import functools

import jax
import jax.numpy as jnp
from jax import lax
from jax.experimental import pallas as pl
from jax.experimental.pallas import tpu as pltpu
from jax.sharding import Mesh
from jax.sharding import PartitionSpec as P

SITE = 16
ITERS = 2
SEC = ("sec_0", "sec_1", "sec_2")
SEC_ROW = ("sec_0", "sec_1", "sec_2", "row")
WINDOW = 32

chemical = 0.4
highest = lax.Precision.HIGHEST


def from_partner(value, axis, distance):
    mask = 2**distance
    pairs = [(source, source ^ mask) for source in range(lax.axis_size(axis))]
    return lax.ppermute(value, axis, pairs)


def dot_over(left, right, left_dim, right_dim, precision=None):
    return lax.dot_general(
        left,
        right,
        (((left_dim,), (right_dim,)), ((), ())),
        precision=precision,
        preferred_element_type=jnp.float32,
    )


def two_parts(values):
    high = values.astype(jnp.bfloat16)
    low = (values - high.astype(jnp.float32)).astype(jnp.bfloat16)
    return high, low


def one_hot(shape, row_key, col_key):
    rows = lax.broadcasted_iota(jnp.int32, shape, 0)
    cols = lax.broadcasted_iota(jnp.int32, shape, 1)
    return row_key(rows) == col_key(cols)


def as_weights(mask):
    return jnp.where(mask, 1.0, 0.0).astype(jnp.bfloat16)


def lower_inverse(grams, window):
    n = grams[0].shape[0]
    lane = lax.broadcasted_iota(jnp.int32, (8, n), 1)
    sub = lax.broadcasted_iota(jnp.int32, (8, n), 0)
    spots = [jnp.full((8, n), m, jnp.int32) for m in range(8)]
    rows = [[g[8 * q : 8 * q + 8, :] for q in range(n // 8)] for g in grams]
    span = window // 8
    for first in range(0, n // 8, span):
        last = first + span
        for q in range(first, last):
            k = 8 * q
            inside = (lane >= k) & (lane < k + 8)
            unit = (lane - k == sub).astype(jnp.float32)
            for mat in rows:
                cols = {
                    r: [jnp.take_along_axis(mat[r], spots[m] + k, axis=1) for m in range(8)]
                    for r in range(q, last)
                }
                for r in range(q, last):
                    mat[r] = jnp.where(inside, unit if r == q else 0.0, mat[r])
                pivot = jnp.broadcast_to(cols[q][0][0:1, :], (8, n))
                for m in range(8):
                    scale = lax.rsqrt(pivot)
                    weights = {
                        j: jnp.broadcast_to(cols[q][m][j : j + 1, :], (8, n)) * scale
                        for j in range(m + 1, 8)
                    }
                    if m < 7:
                        ahead = jnp.broadcast_to(cols[q][m + 1][m + 1 : m + 2, :], (8, n))
                        pivot = ahead - weights[m + 1] * weights[m + 1]
                    below = {r: cols[r][m] * scale for r in range(q, last)}
                    head = jnp.broadcast_to(mat[q][m : m + 1, :], (8, n)) * scale
                    for j in range(m + 1, 8):
                        for r in range(q, last):
                            cols[r][j] = cols[r][j] - below[r] * weights[j]
                    below[q] = jnp.where(sub > m, below[q], 0.0)
                    for r in range(q, last):
                        mat[r] = mat[r] - below[r] * head
                    mat[q] = jnp.where(sub == m, head, mat[q])
        if last < n // 8:
            inblock = (lane >= 8 * first) & (lane < 8 * last)
            for mat in rows:
                panel = jnp.concatenate(mat[first:last], axis=0)
                panel_row = lax.broadcasted_iota(jnp.int32, panel.shape, 0) + 8 * first
                panel_lane = lax.broadcasted_iota(jnp.int32, panel.shape, 1)
                panel = jnp.where((panel_lane > panel_row) & (panel_lane < 8 * last), 0.0, panel)
                update = dot_over(panel, panel, 0, 0, highest)
                for r in range(last, n // 8):
                    mat[r] = jnp.where(inblock, 0.0, mat[r]) - update[8 * r : 8 * r + 8, :]
    full_row = lax.broadcasted_iota(jnp.int32, (n, n), 0)
    full_col = lax.broadcasted_iota(jnp.int32, (n, n), 1)
    return [jnp.where(full_col <= full_row, jnp.concatenate(mat, axis=0), 0.0) for mat in rows]


def three_pass(left, right, right_dim):
    (left_high, left_low), (right_high, right_low) = left, right
    return (
        dot_over(left_high, right_high, 1, right_dim)
        + dot_over(left_high, right_low, 1, right_dim)
        + dot_over(left_low, right_high, 1, right_dim)
    )


def right_kernel(
    slot, rows, place_ref, right_ref, right_ops_ref, high_ref, low_ref, local_ref,
    right_mix, gated, right, sem,
):
    states = right.shape[0]
    terms = gated.shape[0] // states
    wide = SITE * SITE
    local_cols = local_ref.shape[1]
    fetch = pltpu.make_async_copy(right_ref.at[slot], right, sem)
    fetch.start()
    spread = as_weights(one_hot((terms * wide, terms * SITE), lambda r: r // SITE, lambda c: c))
    widen = as_weights(one_hot((SITE, wide), lambda r: r, lambda c: c // SITE))
    same = one_hot((terms * wide, wide), lambda r: r % SITE, lambda c: c % SITE)
    for part, piece in enumerate(two_parts(right_ops_ref[...])):
        tall = dot_over(spread, piece, 1, 0).astype(jnp.bfloat16)
        full = dot_over(tall, widen, 1, 0)
        right_mix[:, part * wide : (part + 1) * wide] = jnp.where(same, full, 0.0).astype(
            jnp.bfloat16
        )
    fetch.wait()
    for pair in range(states // (2 * SITE)):
        base = pair * 2 * SITE
        halves = [
            jnp.concatenate(
                [
                    right[base + h * SITE : base + (h + 1) * SITE, j * states : (j + 1) * states]
                    for j in range(SITE)
                ],
                axis=0,
            )
            for h in range(2)
        ]
        block = jnp.concatenate(halves, axis=1)
        block = jnp.concatenate([block, block], axis=0)
        for t in range(terms):
            mixed = dot_over(right_mix[t * wide : (t + 1) * wide, :], block, 1, 0)
            mixed = mixed.astype(jnp.bfloat16)
            for h in range(2):
                for i in range(SITE):
                    gated[
                        t * states + base + h * SITE : t * states + base + (h + 1) * SITE,
                        i * states : (i + 1) * states,
                    ] = mixed[i * SITE : (i + 1) * SITE, h * states : (h + 1) * states]
    high_ref[...], low_ref[...] = two_parts(dot_over(gated[...], gated[...], 1, 1))
    offset = pl.multiple_of(lax.rem(place_ref[0], rows) * local_cols, local_cols)
    local_ref[...] = gated[:, pl.ds(offset, local_cols)]


def build_left_mix(left_ops_ref, left_mix):
    terms, _, wide = left_mix.shape
    tall_pick = as_weights(one_hot((wide, SITE), lambda r: r % SITE, lambda c: c))
    wide_pick = as_weights(one_hot((SITE, wide), lambda r: r, lambda c: c % SITE))
    group = one_hot((wide, wide), lambda r: r // SITE, lambda c: c // SITE)
    for t in range(terms):
        for part, piece in enumerate(two_parts(left_ops_ref[t])):
            tall = dot_over(tall_pick, piece, 1, 1).astype(jnp.bfloat16)
            full = dot_over(tall, wide_pick, 1, 0)
            left_mix[t, part * wide : (part + 1) * wide, :] = jnp.where(group, full, 0.0).astype(
                jnp.bfloat16
            )


def gate_chunk(left_ref, live, first_row, left_mix_ref, gated, out_first):
    chunk_rows, states = left_ref.shape
    terms, _, wide = left_mix_ref.shape
    turned = left_ref[...].T
    pieces = []
    for b in range(chunk_rows // wide):
        lane = lax.broadcasted_iota(jnp.int32, (states, wide), 1)
        alive = lane < live * SITE - (first_row + b * wide)
        piece = turned[:, b * wide : (b + 1) * wide].astype(jnp.float32)
        pieces.append(jnp.where(alive, piece, 0.0).astype(jnp.bfloat16))
    tall = jnp.concatenate(pieces, axis=0)
    tall = jnp.concatenate([tall, tall], axis=1)
    for t in range(terms):
        mixed = dot_over(tall, left_mix_ref[t], 1, 0).astype(jnp.bfloat16)
        for b in range(len(pieces)):
            gated[
                t * states : (t + 1) * states, out_first + b * wide : out_first + (b + 1) * wide
            ] = mixed[b * states : (b + 1) * states, :]


def gate_sector(row, live, left_refs, left_mix, gated):
    chunks = len(left_refs)
    chunk_rows = left_refs[0].shape[0]
    for c in range(chunks):
        first_row = lax.rem(row + (chunks - c), chunks) * chunk_rows
        gate_chunk(left_refs[c], live, first_row, left_mix, gated, c * chunk_rows)
    return two_parts(dot_over(gated[...], gated[...], 1, 1))


def place(place_ref, rows, slots, sectors):
    row = lax.rem(place_ref[0], rows)
    right_first = lax.div(place_ref[0], rows) * slots
    return row, lax.rem(right_first + sectors // 2, sectors), right_first


def weight_of(charges_ref, sector):
    charge = charges_ref[sector].astype(jnp.float32)
    return jnp.exp(jnp.full((1, 1), -chemical * charge, jnp.float32))


def left_kernel(slots, place_ref, live_ref, left_ops_ref, *refs):
    left_refs = refs[:-5]
    row, left_first, _ = place(place_ref, len(left_refs), slots, live_ref.shape[0])
    own_ref, high_ref, low_ref, left_mix, gated = refs[-5:]
    build_left_mix(left_ops_ref, left_mix)
    high_ref[...], low_ref[...] = gate_sector(
        row, live_ref[left_first], left_refs, left_mix, gated
    )
    own_ref[...] = gated[:, : own_ref.shape[1]]


def krylov_kernel(place_ref, live_ref, kept_ref, charges_ref, *refs):
    chunks = len(refs) - 16
    left_refs = refs[:chunks]
    (left_mix, first_own, first_high, first_low, start_ref) = refs[chunks : chunks + 5]
    square_refs = refs[chunks + 5 : chunks + 9]
    (basis_ref, image_ref) = refs[chunks + 9 : chunks + 11]
    (gated, second_high, second_low, block, final) = refs[chunks + 11 :]
    slots, keep, bond = image_ref.shape
    chunk_rows = left_refs[0].shape[0]
    row, left_first, right_first = place(place_ref, chunks, slots, live_ref.shape[0])
    second_high[...], second_low[...] = gate_sector(
        row, live_ref[left_first + 1], left_refs, left_mix, gated
    )
    gram_refs = ((first_high, first_low), (second_high, second_low))
    for s in range(slots):
        columns = start_ref[pl.ds(left_first + s, 1), :].astype(jnp.float32)
        columns = jnp.broadcast_to(columns, (8, keep)).T[:, :1]
        spots = lax.broadcasted_iota(jnp.int32, (keep, bond), 1).astype(jnp.float32)
        block[s] = jnp.where(spots == columns, 1.0, 0.0)
    weights = [weight_of(charges_ref, right_first + s) for s in range(slots)]

    def step(index, carry):
        images = [
            three_pass(two_parts(block[s]), (gram_refs[s][0][...], gram_refs[s][1][...]), 0)
            for s in range(slots)
        ]
        grams = [dot_over(images[s], block[s], 1, 1, highest) for s in range(slots)]
        inverses = [two_parts(inverse) for inverse in lower_inverse(grams, WINDOW)]
        for s in range(slots):
            image_ref[s] = three_pass(inverses[s], two_parts(images[s]), 0)

        @pl.when(index == ITERS)
        def _():
            for s in range(slots):
                final[s] = three_pass(inverses[s], two_parts(block[s]), 0)

        @pl.when(index < ITERS)
        def _():
            for s in range(slots):
                squares = (square_refs[2 * s][...], square_refs[2 * s + 1][...])
                scale = weights[s] * weights[s]
                block[s] = scale * three_pass(two_parts(image_ref[s]), squares, 0)

        return carry

    lax.fori_loop(0, ITERS + 1, step, 0)
    for s, rows in enumerate((first_own[...], gated[:, :chunk_rows])):
        high, low = two_parts(final[s])
        basis = dot_over(high, rows, 1, 0) + dot_over(low, rows, 1, 0)
        keeps = lax.broadcasted_iota(jnp.int32, basis.shape, 0) < kept_ref[right_first + s]
        basis_ref[s] = jnp.where(keeps, basis, 0.0).T.astype(jnp.bfloat16)


def truncate_kernel(rows, place_ref, kept_ref, charges_ref, image_ref, *refs):
    _, _, right_first = place(place_ref, rows, image_ref.shape[0], kept_ref.shape[0])
    square_refs, local_refs, (right_ref, total_ref) = refs[:4], refs[4:6], refs[6:]
    total = jnp.zeros((1, 1), jnp.float32)
    for s in range(image_ref.shape[0]):
        image = image_ref[s]
        high, low = two_parts(image)
        kept = kept_ref[right_first + s]
        weight = weight_of(charges_ref, right_first + s)
        keeps = lax.broadcasted_iota(jnp.int32, image.shape, 0) < kept
        scale = weight * weight
        squares = (square_refs[2 * s][...], square_refs[2 * s + 1][...])
        squared = scale * three_pass((high, low), squares, 0) * image
        squared = jnp.where(keeps, squared, 0.0)
        total += jnp.sum(jnp.sum(squared, axis=0, keepdims=True), axis=1, keepdims=True)
        local = local_refs[s][...]
        part = dot_over(high, local, 1, 0) + dot_over(low, local, 1, 0)
        keeps = lax.broadcasted_iota(jnp.int32, part.shape, 0) < kept
        right_ref[s] = jnp.where(keeps, part * weight, 0.0)
    total_ref[...] = jnp.broadcast_to(total, total_ref.shape)


def finish_kernel(totals_ref, part_ref, sent_ref, basis_ref, right_ref):
    basis_ref[...] = sent_ref[...].astype(jnp.float32)
    total = jnp.sum(totals_ref[...], axis=0, keepdims=True)[:, :1]
    factor = 1.0 / jnp.sqrt(total)
    for s in range(part_ref.shape[0]):
        right_ref[s] = part_ref[s] * factor


def smem():
    return pl.BlockSpec(memory_space=pltpu.SMEM)


def vmem():
    return pl.BlockSpec(memory_space=pltpu.VMEM)


def shape_of(shape, dtype):
    return jax.ShapeDtypeStruct(shape, dtype)


def kernel_options(mebibytes, flops):
    return dict(
        compiler_params=pltpu.CompilerParams(vmem_limit_bytes=mebibytes << 20),
        cost_estimate=pl.CostEstimate(flops=int(flops), bytes_accessed=2 << 20, transcendentals=0),
    )


def gate_right(slot, row, right_block, right_ops, local_cols):
    _, states, cols = right_block.shape
    terms = right_ops.shape[0]
    bond, wide = terms * states, SITE * SITE
    return pl.pallas_call(
        functools.partial(right_kernel, slot, cols // local_cols),
        in_specs=[smem(), pl.BlockSpec(memory_space=pltpu.HBM), vmem()],
        out_specs=[vmem()] * 3,
        out_shape=[
            shape_of((bond, bond), jnp.bfloat16),
            shape_of((bond, bond), jnp.bfloat16),
            shape_of((bond, local_cols), jnp.bfloat16),
        ],
        scratch_shapes=[
            pltpu.VMEM((terms * wide, 2 * wide), jnp.bfloat16),
            pltpu.VMEM((bond, cols), jnp.bfloat16),
            pltpu.VMEM((states, cols), jnp.bfloat16),
            pltpu.SemaphoreType.DMA,
        ],
        name="right_gate",
        **kernel_options(12, 4e9),
    )(row, right_block, right_ops.reshape(terms * SITE, SITE))


def gate_left(slots, row, live, left_chunks, left_ops):
    chunk_rows, states = left_chunks[0].shape
    terms = left_ops.shape[0]
    bond, wide = terms * states, SITE * SITE
    return pl.pallas_call(
        functools.partial(left_kernel, slots),
        in_specs=[smem()] * 2 + [vmem()] * (1 + len(left_chunks)),
        out_specs=[vmem()] * 4,
        out_shape=[
            shape_of((bond, chunk_rows), jnp.bfloat16),
            shape_of((bond, bond), jnp.bfloat16),
            shape_of((bond, bond), jnp.bfloat16),
            shape_of((terms, 2 * wide, wide), jnp.bfloat16),
        ],
        scratch_shapes=[pltpu.VMEM((bond, len(left_chunks) * chunk_rows), jnp.bfloat16)],
        name="left_gate",
        **kernel_options(10, 4e9),
    )(row, live, left_ops, *left_chunks)


def krylov_part(slots, row, live, kept, charges, left_chunks, left_mix, first, start, squares):
    chunk_rows, _ = left_chunks[0].shape
    bond = squares[0].shape[0]
    keep = start.shape[1]
    return pl.pallas_call(
        krylov_kernel,
        in_specs=[smem()] * 4 + [vmem()] * (len(left_chunks) + 2 + len(first) + len(squares)),
        out_specs=[vmem()] * 2,
        out_shape=[
            shape_of((slots, chunk_rows, keep), jnp.bfloat16),
            shape_of((slots, keep, bond), jnp.float32),
        ],
        scratch_shapes=[
            pltpu.VMEM((bond, len(left_chunks) * chunk_rows), jnp.bfloat16),
            pltpu.VMEM((bond, bond), jnp.bfloat16),
            pltpu.VMEM((bond, bond), jnp.bfloat16),
            pltpu.VMEM((slots, keep, bond), jnp.float32),
            pltpu.VMEM((slots, keep, bond), jnp.float32),
        ],
        name="krylov",
        **kernel_options(14, 2e10),
    )(row, live, kept, charges, *left_chunks, left_mix, *first, start, *squares)


def truncated(rows, row, kept, charges, image, squares, locals_, peers):
    slots, keep, _ = image.shape
    local_cols = locals_[0].shape[1]
    return pl.pallas_call(
        functools.partial(truncate_kernel, rows),
        in_specs=[smem()] * 3 + [vmem()] * (1 + len(squares) + len(locals_)),
        out_specs=[vmem()] * 2,
        out_shape=[
            shape_of((slots, keep, local_cols), jnp.float32),
            shape_of((peers, keep), jnp.float32),
        ],
        name="truncate",
        **kernel_options(8, 2e9),
    )(row, kept, charges, image, *squares, *locals_)


def finished(totals, part, sent):
    return pl.pallas_call(
        finish_kernel,
        in_specs=[vmem()] * 3,
        out_specs=[vmem()] * 2,
        out_shape=[shape_of(sent.shape, jnp.float32), shape_of(part.shape, jnp.float32)],
        name="finish",
        **kernel_options(4, 1e6),
    )(totals, part, sent)


def on_device(left_block, right_block, left_ops, right_ops, charges, live_states, kept, start):
    slots = left_block.shape[0]
    top_bit = lax.axis_size(SEC).bit_length() - 2
    row = lax.axis_index(SEC_ROW).astype(jnp.int32).reshape(1)
    local_cols = right_block.shape[2] // lax.axis_size("row")
    rows = lax.axis_size("row")

    def over_rows(chunk):
        sent = [
            lax.ppermute(chunk, "row", [(i, (i + d) % rows) for i in range(rows)])
            for d in range(1, rows)
        ]
        return [chunk, *sent]

    theirs = [from_partner(left_block[s], SEC, top_bit) for s in range(slots)]
    first = list(gate_right(0, row, right_block, right_ops, local_cols))
    theirs[0], first[0], row_second = lax.optimization_barrier((theirs[0], first[0], row))
    first_chunks = over_rows(theirs[0])
    second = list(gate_right(1, row_second, right_block, right_ops, local_cols))
    theirs[1], second[0], row_left = lax.optimization_barrier((theirs[1], second[0], row))
    second_chunks = over_rows(theirs[1])
    *first_left, left_mix = gate_left(slots, row_left, live_states, first_chunks, left_ops)
    squares = (*first[:2], *second[:2])
    basis, image = krylov_part(
        slots, row, live_states, kept, charges, second_chunks, left_mix, first_left, start, squares
    )
    basis = from_partner(basis, SEC, top_bit)
    right_part, total = truncated(
        rows, row, kept, charges, image, squares, (first[2], second[2]), lax.axis_size(SEC)
    )
    totals = lax.all_to_all(total, SEC, split_axis=0, concat_axis=0, tiled=True)
    return tuple(finished(totals, right_part, basis))


def solution(mesh):
    finer = Mesh(
        mesh.devices.reshape(8, 4, 2, mesh.shape["row"]), ("sec_0", "sec_1", "sec_2", "row")
    )
    in_specs = (P(SEC, "row", None), P(SEC, None, None), P(), P(), P(), P(), P(), P())
    out_specs = (P(SEC, "row", None), P(SEC, None, "row"))
    return jax.shard_map(
        on_device, mesh=finer, in_specs=in_specs, out_specs=out_specs, check_vma=False
    )
```

```python
import functools

import jax
import jax.numpy as jnp
from jax import lax
from jax.experimental import pallas as pl
from jax.experimental.pallas import tpu as pltpu
from jax.sharding import Mesh
from jax.sharding import PartitionSpec as P

SITE = 16
ITERS = 2
SEC = ("sec_0", "sec_1", "sec_2")
SEC_ROW = ("sec_0", "sec_1", "sec_2", "row")
WINDOW = 32

chemical = 0.4
highest = lax.Precision.HIGHEST


def from_partner(value, axis, distance):
    mask = 2**distance
    pairs = [(source, source ^ mask) for source in range(lax.axis_size(axis))]
    return lax.ppermute(value, axis, pairs)


def dot_over(left, right, left_dim, right_dim, precision=None):
    return lax.dot_general(
        left,
        right,
        (((left_dim,), (right_dim,)), ((), ())),
        precision=precision,
        preferred_element_type=jnp.float32,
    )


def two_parts(values):
    high = values.astype(jnp.bfloat16)
    low = (values - high.astype(jnp.float32)).astype(jnp.bfloat16)
    return high, low


def one_hot(shape, row_key, col_key):
    rows = lax.broadcasted_iota(jnp.int32, shape, 0)
    cols = lax.broadcasted_iota(jnp.int32, shape, 1)
    return row_key(rows) == col_key(cols)


def as_weights(mask):
    return jnp.where(mask, 1.0, 0.0).astype(jnp.bfloat16)


def lower_inverse(grams, window):
    n = grams[0].shape[0]
    lane = lax.broadcasted_iota(jnp.int32, (8, n), 1)
    sub = lax.broadcasted_iota(jnp.int32, (8, n), 0)
    spots = [jnp.full((8, n), m, jnp.int32) for m in range(8)]
    rows = [[g[8 * q : 8 * q + 8, :] for q in range(n // 8)] for g in grams]
    span = window // 8
    for first in range(0, n // 8, span):
        last = first + span
        for q in range(first, last):
            k = 8 * q
            inside = (lane >= k) & (lane < k + 8)
            unit = (lane - k == sub).astype(jnp.float32)
            for mat in rows:
                cols = {
                    r: [jnp.take_along_axis(mat[r], spots[m] + k, axis=1) for m in range(8)]
                    for r in range(q, last)
                }
                for r in range(q, last):
                    mat[r] = jnp.where(inside, unit if r == q else 0.0, mat[r])
                pivot = jnp.broadcast_to(cols[q][0][0:1, :], (8, n))
                for m in range(8):
                    scale = lax.rsqrt(pivot)
                    weights = {
                        j: jnp.broadcast_to(cols[q][m][j : j + 1, :], (8, n)) * scale
                        for j in range(m + 1, 8)
                    }
                    if m < 7:
                        ahead = jnp.broadcast_to(cols[q][m + 1][m + 1 : m + 2, :], (8, n))
                        pivot = ahead - weights[m + 1] * weights[m + 1]
                    below = {r: cols[r][m] * scale for r in range(q, last)}
                    head = jnp.broadcast_to(mat[q][m : m + 1, :], (8, n)) * scale
                    for j in range(m + 1, 8):
                        for r in range(q, last):
                            cols[r][j] = cols[r][j] - below[r] * weights[j]
                    below[q] = jnp.where(sub > m, below[q], 0.0)
                    for r in range(q, last):
                        mat[r] = mat[r] - below[r] * head
                    mat[q] = jnp.where(sub == m, head, mat[q])
        if last < n // 8:
            inblock = (lane >= 8 * first) & (lane < 8 * last)
            for mat in rows:
                panel = jnp.concatenate(mat[first:last], axis=0)
                panel_row = lax.broadcasted_iota(jnp.int32, panel.shape, 0) + 8 * first
                panel_lane = lax.broadcasted_iota(jnp.int32, panel.shape, 1)
                panel = jnp.where((panel_lane > panel_row) & (panel_lane < 8 * last), 0.0, panel)
                update = dot_over(panel, panel, 0, 0, highest)
                for r in range(last, n // 8):
                    mat[r] = jnp.where(inblock, 0.0, mat[r]) - update[8 * r : 8 * r + 8, :]
    full_row = lax.broadcasted_iota(jnp.int32, (n, n), 0)
    full_col = lax.broadcasted_iota(jnp.int32, (n, n), 1)
    return [jnp.where(full_col <= full_row, jnp.concatenate(mat, axis=0), 0.0) for mat in rows]


def three_pass(left, right, right_dim):
    (left_high, left_low), (right_high, right_low) = left, right
    return (
        dot_over(left_high, right_high, 1, right_dim)
        + dot_over(left_high, right_low, 1, right_dim)
        + dot_over(left_low, right_high, 1, right_dim)
    )


def right_kernel(rows, place_ref, right_ref, right_ops_ref, *refs):
    *out_refs, right_mix, gated, right, sems = refs
    slots, states = right.shape[:2]
    terms = gated.shape[0] // states
    wide = SITE * SITE
    fetches = [
        pltpu.make_async_copy(right_ref.at[s], right.at[s], sems.at[s]) for s in range(slots)
    ]
    for fetch in fetches:
        fetch.start()
    spread = as_weights(one_hot((terms * wide, terms * SITE), lambda r: r // SITE, lambda c: c))
    widen = as_weights(one_hot((SITE, wide), lambda r: r, lambda c: c // SITE))
    same = one_hot((terms * wide, wide), lambda r: r % SITE, lambda c: c % SITE)
    for part, piece in enumerate(two_parts(right_ops_ref[...])):
        tall = dot_over(spread, piece, 1, 0).astype(jnp.bfloat16)
        full = dot_over(tall, widen, 1, 0)
        right_mix[:, part * wide : (part + 1) * wide] = jnp.where(same, full, 0.0).astype(
            jnp.bfloat16
        )
    for s in range(slots):
        high_ref, low_ref, local_ref = out_refs[3 * s : 3 * s + 3]
        local_cols = local_ref.shape[1]
        fetches[s].wait()
        for pair in range(states // (2 * SITE)):
            base = pair * 2 * SITE
            halves = [
                jnp.concatenate(
                    [
                        right[
                            s,
                            base + h * SITE : base + (h + 1) * SITE,
                            j * states : (j + 1) * states,
                        ]
                        for j in range(SITE)
                    ],
                    axis=0,
                )
                for h in range(2)
            ]
            block = jnp.concatenate(halves, axis=1)
            block = jnp.concatenate([block, block], axis=0)
            for t in range(terms):
                mixed = dot_over(right_mix[t * wide : (t + 1) * wide, :], block, 1, 0)
                mixed = mixed.astype(jnp.bfloat16)
                for h in range(2):
                    for i in range(SITE):
                        gated[
                            t * states + base + h * SITE : t * states + base + (h + 1) * SITE,
                            i * states : (i + 1) * states,
                        ] = mixed[i * SITE : (i + 1) * SITE, h * states : (h + 1) * states]
        high_ref[...], low_ref[...] = two_parts(dot_over(gated[...], gated[...], 1, 1))
        offset = pl.multiple_of(lax.rem(place_ref[0], rows) * local_cols, local_cols)
        local_ref[...] = gated[:, pl.ds(offset, local_cols)]


def build_left_mix(left_ops_ref, left_mix):
    terms, _, wide = left_mix.shape
    tall_pick = as_weights(one_hot((wide, SITE), lambda r: r % SITE, lambda c: c))
    wide_pick = as_weights(one_hot((SITE, wide), lambda r: r, lambda c: c % SITE))
    group = one_hot((wide, wide), lambda r: r // SITE, lambda c: c // SITE)
    for t in range(terms):
        for part, piece in enumerate(two_parts(left_ops_ref[t])):
            tall = dot_over(tall_pick, piece, 1, 1).astype(jnp.bfloat16)
            full = dot_over(tall, wide_pick, 1, 0)
            left_mix[t, part * wide : (part + 1) * wide, :] = jnp.where(group, full, 0.0).astype(
                jnp.bfloat16
            )


def gate_chunk(left_ref, live, first_row, left_mix_ref, gated, out_first):
    chunk_rows, states = left_ref.shape
    terms, _, wide = left_mix_ref.shape
    turned = left_ref[...].T
    pieces = []
    for b in range(chunk_rows // wide):
        lane = lax.broadcasted_iota(jnp.int32, (states, wide), 1)
        alive = lane < live * SITE - (first_row + b * wide)
        piece = turned[:, b * wide : (b + 1) * wide].astype(jnp.float32)
        pieces.append(jnp.where(alive, piece, 0.0).astype(jnp.bfloat16))
    tall = jnp.concatenate(pieces, axis=0)
    tall = jnp.concatenate([tall, tall], axis=1)
    for t in range(terms):
        mixed = dot_over(tall, left_mix_ref[t], 1, 0).astype(jnp.bfloat16)
        for b in range(len(pieces)):
            gated[
                t * states : (t + 1) * states, out_first + b * wide : out_first + (b + 1) * wide
            ] = mixed[b * states : (b + 1) * states, :]


def gate_sector(row, live, left_refs, left_mix, gated):
    chunks = len(left_refs)
    chunk_rows = left_refs[0].shape[0]
    for c in range(chunks):
        first_row = lax.rem(row + (chunks - c), chunks) * chunk_rows
        gate_chunk(left_refs[c], live, first_row, left_mix, gated, c * chunk_rows)
    return two_parts(dot_over(gated[...], gated[...], 1, 1))


def place(place_ref, rows, slots, sectors):
    row = lax.rem(place_ref[0], rows)
    right_first = lax.div(place_ref[0], rows) * slots
    return row, lax.rem(right_first + sectors // 2, sectors), right_first


def weight_of(charges_ref, sector):
    charge = charges_ref[sector].astype(jnp.float32)
    return jnp.exp(jnp.full((1, 1), -chemical * charge, jnp.float32))


def left_kernel(slots, place_ref, live_ref, left_ops_ref, *refs):
    left_refs = refs[:-5]
    row, left_first, _ = place(place_ref, len(left_refs), slots, live_ref.shape[0])
    own_ref, high_ref, low_ref, left_mix, gated = refs[-5:]
    build_left_mix(left_ops_ref, left_mix)
    high_ref[...], low_ref[...] = gate_sector(
        row, live_ref[left_first], left_refs, left_mix, gated
    )
    own_ref[...] = gated[:, : own_ref.shape[1]]


def krylov_kernel(place_ref, live_ref, kept_ref, charges_ref, *refs):
    chunks = len(refs) - 16
    left_refs = refs[:chunks]
    (left_mix, first_own, first_high, first_low, start_ref) = refs[chunks : chunks + 5]
    square_refs = refs[chunks + 5 : chunks + 9]
    (basis_ref, image_ref) = refs[chunks + 9 : chunks + 11]
    (gated, second_high, second_low, block, final) = refs[chunks + 11 :]
    slots, keep, bond = image_ref.shape
    chunk_rows = left_refs[0].shape[0]
    row, left_first, right_first = place(place_ref, chunks, slots, live_ref.shape[0])
    second_high[...], second_low[...] = gate_sector(
        row, live_ref[left_first + 1], left_refs, left_mix, gated
    )
    gram_refs = ((first_high, first_low), (second_high, second_low))
    for s in range(slots):
        columns = start_ref[pl.ds(left_first + s, 1), :].astype(jnp.float32)
        columns = jnp.broadcast_to(columns, (8, keep)).T[:, :1]
        spots = lax.broadcasted_iota(jnp.int32, (keep, bond), 1).astype(jnp.float32)
        block[s] = jnp.where(spots == columns, 1.0, 0.0)
    weights = [weight_of(charges_ref, right_first + s) for s in range(slots)]

    def step(index, carry):
        images = [
            three_pass(two_parts(block[s]), (gram_refs[s][0][...], gram_refs[s][1][...]), 0)
            for s in range(slots)
        ]
        grams = [dot_over(images[s], block[s], 1, 1, highest) for s in range(slots)]
        inverses = [two_parts(inverse) for inverse in lower_inverse(grams, WINDOW)]
        for s in range(slots):
            image_ref[s] = three_pass(inverses[s], two_parts(images[s]), 0)

        @pl.when(index == ITERS)
        def _():
            for s in range(slots):
                final[s] = three_pass(inverses[s], two_parts(block[s]), 0)

        @pl.when(index < ITERS)
        def _():
            for s in range(slots):
                squares = (square_refs[2 * s][...], square_refs[2 * s + 1][...])
                scale = weights[s] * weights[s]
                block[s] = scale * three_pass(two_parts(image_ref[s]), squares, 0)

        return carry

    lax.fori_loop(0, ITERS + 1, step, 0)
    for s, rows in enumerate((first_own[...], gated[:, :chunk_rows])):
        high, low = two_parts(final[s])
        basis = dot_over(high, rows, 1, 0) + dot_over(low, rows, 1, 0)
        keeps = lax.broadcasted_iota(jnp.int32, basis.shape, 0) < kept_ref[right_first + s]
        basis_ref[s] = jnp.where(keeps, basis, 0.0).T.astype(jnp.bfloat16)


def truncate_kernel(rows, place_ref, kept_ref, charges_ref, image_ref, *refs):
    _, _, right_first = place(place_ref, rows, image_ref.shape[0], kept_ref.shape[0])
    square_refs, local_refs, (right_ref, total_ref) = refs[:4], refs[4:6], refs[6:]
    total = jnp.zeros((1, 1), jnp.float32)
    for s in range(image_ref.shape[0]):
        image = image_ref[s]
        high, low = two_parts(image)
        kept = kept_ref[right_first + s]
        weight = weight_of(charges_ref, right_first + s)
        keeps = lax.broadcasted_iota(jnp.int32, image.shape, 0) < kept
        scale = weight * weight
        squares = (square_refs[2 * s][...], square_refs[2 * s + 1][...])
        squared = scale * three_pass((high, low), squares, 0) * image
        squared = jnp.where(keeps, squared, 0.0)
        total += jnp.sum(jnp.sum(squared, axis=0, keepdims=True), axis=1, keepdims=True)
        local = local_refs[s][...]
        part = dot_over(high, local, 1, 0) + dot_over(low, local, 1, 0)
        keeps = lax.broadcasted_iota(jnp.int32, part.shape, 0) < kept
        right_ref[s] = jnp.where(keeps, part * weight, 0.0)
    total_ref[...] = jnp.broadcast_to(total, total_ref.shape)


def finish_kernel(totals_ref, part_ref, sent_ref, basis_ref, right_ref):
    basis_ref[...] = sent_ref[...].astype(jnp.float32)
    total = jnp.sum(totals_ref[...], axis=0, keepdims=True)[:, :1]
    factor = 1.0 / jnp.sqrt(total)
    for s in range(part_ref.shape[0]):
        right_ref[s] = part_ref[s] * factor


def smem():
    return pl.BlockSpec(memory_space=pltpu.SMEM)


def vmem():
    return pl.BlockSpec(memory_space=pltpu.VMEM)


def shape_of(shape, dtype):
    return jax.ShapeDtypeStruct(shape, dtype)


def kernel_options(mebibytes, flops):
    return dict(
        compiler_params=pltpu.CompilerParams(vmem_limit_bytes=mebibytes << 20),
        cost_estimate=pl.CostEstimate(flops=int(flops), bytes_accessed=2 << 20, transcendentals=0),
    )


def gate_right(row, right_block, right_ops, local_cols):
    slots, states, cols = right_block.shape
    terms = right_ops.shape[0]
    bond, wide = terms * states, SITE * SITE
    return pl.pallas_call(
        functools.partial(right_kernel, cols // local_cols),
        in_specs=[smem(), pl.BlockSpec(memory_space=pltpu.HBM), vmem()],
        out_specs=[vmem()] * (3 * slots),
        out_shape=[
            shape_of((bond, bond), jnp.bfloat16),
            shape_of((bond, bond), jnp.bfloat16),
            shape_of((bond, local_cols), jnp.bfloat16),
        ]
        * slots,
        scratch_shapes=[
            pltpu.VMEM((terms * wide, 2 * wide), jnp.bfloat16),
            pltpu.VMEM((bond, cols), jnp.bfloat16),
            pltpu.VMEM((slots, states, cols), jnp.bfloat16),
            pltpu.SemaphoreType.DMA((slots,)),
        ],
        name="right_gate",
        **kernel_options(12, 8e9),
    )(row, right_block, right_ops.reshape(terms * SITE, SITE))


def gate_left(slots, row, live, left_chunks, left_ops):
    chunk_rows, states = left_chunks[0].shape
    terms = left_ops.shape[0]
    bond, wide = terms * states, SITE * SITE
    return pl.pallas_call(
        functools.partial(left_kernel, slots),
        in_specs=[smem()] * 2 + [vmem()] * (1 + len(left_chunks)),
        out_specs=[vmem()] * 4,
        out_shape=[
            shape_of((bond, chunk_rows), jnp.bfloat16),
            shape_of((bond, bond), jnp.bfloat16),
            shape_of((bond, bond), jnp.bfloat16),
            shape_of((terms, 2 * wide, wide), jnp.bfloat16),
        ],
        scratch_shapes=[pltpu.VMEM((bond, len(left_chunks) * chunk_rows), jnp.bfloat16)],
        name="left_gate",
        **kernel_options(10, 4e9),
    )(row, live, left_ops, *left_chunks)


def krylov_part(slots, row, live, kept, charges, left_chunks, left_mix, first, start, squares):
    chunk_rows, _ = left_chunks[0].shape
    bond = squares[0].shape[0]
    keep = start.shape[1]
    return pl.pallas_call(
        krylov_kernel,
        in_specs=[smem()] * 4 + [vmem()] * (len(left_chunks) + 2 + len(first) + len(squares)),
        out_specs=[vmem()] * 2,
        out_shape=[
            shape_of((slots, chunk_rows, keep), jnp.bfloat16),
            shape_of((slots, keep, bond), jnp.float32),
        ],
        scratch_shapes=[
            pltpu.VMEM((bond, len(left_chunks) * chunk_rows), jnp.bfloat16),
            pltpu.VMEM((bond, bond), jnp.bfloat16),
            pltpu.VMEM((bond, bond), jnp.bfloat16),
            pltpu.VMEM((slots, keep, bond), jnp.float32),
            pltpu.VMEM((slots, keep, bond), jnp.float32),
        ],
        name="krylov",
        **kernel_options(14, 2e10),
    )(row, live, kept, charges, *left_chunks, left_mix, *first, start, *squares)


def truncated(rows, row, kept, charges, image, squares, locals_, peers):
    slots, keep, _ = image.shape
    local_cols = locals_[0].shape[1]
    return pl.pallas_call(
        functools.partial(truncate_kernel, rows),
        in_specs=[smem()] * 3 + [vmem()] * (1 + len(squares) + len(locals_)),
        out_specs=[vmem()] * 2,
        out_shape=[
            shape_of((slots, keep, local_cols), jnp.float32),
            shape_of((peers, keep), jnp.float32),
        ],
        name="truncate",
        **kernel_options(8, 2e9),
    )(row, kept, charges, image, *squares, *locals_)


def finished(totals, part, sent):
    return pl.pallas_call(
        finish_kernel,
        in_specs=[vmem()] * 3,
        out_specs=[vmem()] * 2,
        out_shape=[shape_of(sent.shape, jnp.float32), shape_of(part.shape, jnp.float32)],
        name="finish",
        **kernel_options(4, 1e6),
    )(totals, part, sent)


def on_device(left_block, right_block, left_ops, right_ops, charges, live_states, kept, start):
    slots = left_block.shape[0]
    top_bit = lax.axis_size(SEC).bit_length() - 2
    row = lax.axis_index(SEC_ROW).astype(jnp.int32).reshape(1)
    local_cols = right_block.shape[2] // lax.axis_size("row")
    rows = lax.axis_size("row")

    def over_rows(chunk):
        sent = [
            lax.ppermute(chunk, "row", [(i, (i + d) % rows) for i in range(rows)])
            for d in range(1, rows)
        ]
        return [chunk, *sent]

    theirs = [from_partner(left_block[s], SEC, top_bit) for s in range(slots)]
    right_sides = gate_right(row, right_block, right_ops, local_cols)
    theirs, right_sides = lax.optimization_barrier((theirs, right_sides))
    first, second = right_sides[:3], right_sides[3:]
    first_chunks, second_chunks = over_rows(theirs[0]), over_rows(theirs[1])
    *first_left, left_mix = gate_left(slots, row, live_states, first_chunks, left_ops)
    squares = (*first[:2], *second[:2])
    basis, image = krylov_part(
        slots, row, live_states, kept, charges, second_chunks, left_mix, first_left, start, squares
    )
    basis = from_partner(basis, SEC, top_bit)
    right_part, total = truncated(
        rows, row, kept, charges, image, squares, (first[2], second[2]), lax.axis_size(SEC)
    )
    totals = lax.all_to_all(total, SEC, split_axis=0, concat_axis=0, tiled=True)
    return tuple(finished(totals, right_part, basis))


def solution(mesh):
    finer = Mesh(
        mesh.devices.reshape(8, 4, 2, mesh.shape["row"]), ("sec_0", "sec_1", "sec_2", "row")
    )
    in_specs = (P(SEC, "row", None), P(SEC, None, None), P(), P(), P(), P(), P(), P())
    out_specs = (P(SEC, "row", None), P(SEC, None, "row"))
    return jax.shard_map(
        on_device, mesh=finer, in_specs=in_specs, out_specs=out_specs, check_vma=False
    )
```

```python
import functools

import jax
import jax.numpy as jnp
from jax import lax
from jax.experimental import pallas as pl
from jax.experimental.pallas import tpu as pltpu
from jax.sharding import Mesh
from jax.sharding import PartitionSpec as P

SITE = 16
ITERS = 2
SEC = ("sec_0", "sec_1", "sec_2")
SEC_ROW = ("sec_0", "sec_1", "sec_2", "row")
WINDOW = 32

chemical = 0.4
highest = lax.Precision.HIGHEST


def from_partner(value, axis, distance):
    mask = 2**distance
    pairs = [(source, source ^ mask) for source in range(lax.axis_size(axis))]
    return lax.ppermute(value, axis, pairs)


def dot_over(left, right, left_dim, right_dim, precision=None):
    return lax.dot_general(
        left,
        right,
        (((left_dim,), (right_dim,)), ((), ())),
        precision=precision,
        preferred_element_type=jnp.float32,
    )


def two_parts(values):
    high = values.astype(jnp.bfloat16)
    low = (values - high.astype(jnp.float32)).astype(jnp.bfloat16)
    return high, low


def one_hot(shape, row_key, col_key):
    rows = lax.broadcasted_iota(jnp.int32, shape, 0)
    cols = lax.broadcasted_iota(jnp.int32, shape, 1)
    return row_key(rows) == col_key(cols)


def as_weights(mask):
    return jnp.where(mask, 1.0, 0.0).astype(jnp.bfloat16)


def lower_inverse(grams, window):
    n = grams[0].shape[0]
    lane = lax.broadcasted_iota(jnp.int32, (8, n), 1)
    sub = lax.broadcasted_iota(jnp.int32, (8, n), 0)
    spots = [jnp.full((8, n), m, jnp.int32) for m in range(8)]
    rows = [[g[8 * q : 8 * q + 8, :] for q in range(n // 8)] for g in grams]
    span = window // 8
    for first in range(0, n // 8, span):
        last = first + span
        for q in range(first, last):
            k = 8 * q
            inside = (lane >= k) & (lane < k + 8)
            unit = (lane - k == sub).astype(jnp.float32)
            for mat in rows:
                cols = {
                    r: [jnp.take_along_axis(mat[r], spots[m] + k, axis=1) for m in range(8)]
                    for r in range(q, last)
                }
                for r in range(q, last):
                    mat[r] = jnp.where(inside, unit if r == q else 0.0, mat[r])
                pivot = jnp.broadcast_to(cols[q][0][0:1, :], (8, n))
                for m in range(8):
                    scale = lax.rsqrt(pivot)
                    weights = {
                        j: jnp.broadcast_to(cols[q][m][j : j + 1, :], (8, n)) * scale
                        for j in range(m + 1, 8)
                    }
                    if m < 7:
                        ahead = jnp.broadcast_to(cols[q][m + 1][m + 1 : m + 2, :], (8, n))
                        pivot = ahead - weights[m + 1] * weights[m + 1]
                    below = {r: cols[r][m] * scale for r in range(q, last)}
                    head = jnp.broadcast_to(mat[q][m : m + 1, :], (8, n)) * scale
                    for j in range(m + 1, 8):
                        for r in range(q, last):
                            cols[r][j] = cols[r][j] - below[r] * weights[j]
                    below[q] = jnp.where(sub > m, below[q], 0.0)
                    for r in range(q, last):
                        mat[r] = mat[r] - below[r] * head
                    mat[q] = jnp.where(sub == m, head, mat[q])
        if last < n // 8:
            inblock = (lane >= 8 * first) & (lane < 8 * last)
            for mat in rows:
                panel = jnp.concatenate(mat[first:last], axis=0)
                panel_row = lax.broadcasted_iota(jnp.int32, panel.shape, 0) + 8 * first
                panel_lane = lax.broadcasted_iota(jnp.int32, panel.shape, 1)
                panel = jnp.where((panel_lane > panel_row) & (panel_lane < 8 * last), 0.0, panel)
                update = dot_over(panel, panel, 0, 0, highest)
                for r in range(last, n // 8):
                    mat[r] = jnp.where(inblock, 0.0, mat[r]) - update[8 * r : 8 * r + 8, :]
    full_row = lax.broadcasted_iota(jnp.int32, (n, n), 0)
    full_col = lax.broadcasted_iota(jnp.int32, (n, n), 1)
    return [jnp.where(full_col <= full_row, jnp.concatenate(mat, axis=0), 0.0) for mat in rows]


def three_pass(left, right, right_dim):
    (left_high, left_low), (right_high, right_low) = left, right
    return (
        dot_over(left_high, right_high, 1, right_dim)
        + dot_over(left_high, right_low, 1, right_dim)
        + dot_over(left_low, right_high, 1, right_dim)
    )


def right_kernel(
    slot, rows, place_ref, right_ref, right_ops_ref, high_ref, low_ref, local_ref,
    right_mix, gated, right, sem,
):
    states = right.shape[0]
    terms = gated.shape[0] // states
    wide = SITE * SITE
    local_cols = local_ref.shape[1]
    fetch = pltpu.make_async_copy(right_ref.at[slot], right, sem)
    fetch.start()
    spread = as_weights(one_hot((terms * wide, terms * SITE), lambda r: r // SITE, lambda c: c))
    widen = as_weights(one_hot((SITE, wide), lambda r: r, lambda c: c // SITE))
    same = one_hot((terms * wide, wide), lambda r: r % SITE, lambda c: c % SITE)
    for part, piece in enumerate(two_parts(right_ops_ref[...])):
        tall = dot_over(spread, piece, 1, 0).astype(jnp.bfloat16)
        full = dot_over(tall, widen, 1, 0)
        right_mix[:, part * wide : (part + 1) * wide] = jnp.where(same, full, 0.0).astype(
            jnp.bfloat16
        )
    fetch.wait()
    for pair in range(states // (2 * SITE)):
        base = pair * 2 * SITE
        halves = [
            jnp.concatenate(
                [
                    right[base + h * SITE : base + (h + 1) * SITE, j * states : (j + 1) * states]
                    for j in range(SITE)
                ],
                axis=0,
            )
            for h in range(2)
        ]
        block = jnp.concatenate(halves, axis=1)
        block = jnp.concatenate([block, block], axis=0)
        for t in range(terms):
            mixed = dot_over(right_mix[t * wide : (t + 1) * wide, :], block, 1, 0)
            mixed = mixed.astype(jnp.bfloat16)
            for h in range(2):
                for i in range(SITE):
                    gated[
                        t * states + base + h * SITE : t * states + base + (h + 1) * SITE,
                        i * states : (i + 1) * states,
                    ] = mixed[i * SITE : (i + 1) * SITE, h * states : (h + 1) * states]
    high_ref[...], low_ref[...] = two_parts(dot_over(gated[...], gated[...], 1, 1))
    offset = pl.multiple_of(lax.rem(place_ref[0], rows) * local_cols, local_cols)
    local_ref[...] = gated[:, pl.ds(offset, local_cols)]


def build_left_mix(left_ops_ref, left_mix):
    terms, _, wide = left_mix.shape
    tall_pick = as_weights(one_hot((wide, SITE), lambda r: r % SITE, lambda c: c))
    wide_pick = as_weights(one_hot((SITE, wide), lambda r: r, lambda c: c % SITE))
    group = one_hot((wide, wide), lambda r: r // SITE, lambda c: c // SITE)
    for t in range(terms):
        for part, piece in enumerate(two_parts(left_ops_ref[t])):
            tall = dot_over(tall_pick, piece, 1, 1).astype(jnp.bfloat16)
            full = dot_over(tall, wide_pick, 1, 0)
            left_mix[t, part * wide : (part + 1) * wide, :] = jnp.where(group, full, 0.0).astype(
                jnp.bfloat16
            )


def gate_chunk(left_ref, live, first_row, left_mix_ref, gated, out_first):
    chunk_rows, states = left_ref.shape
    terms, _, wide = left_mix_ref.shape
    turned = left_ref[...].T
    pieces = []
    for b in range(chunk_rows // wide):
        lane = lax.broadcasted_iota(jnp.int32, (states, wide), 1)
        alive = lane < live * SITE - (first_row + b * wide)
        piece = turned[:, b * wide : (b + 1) * wide].astype(jnp.float32)
        pieces.append(jnp.where(alive, piece, 0.0).astype(jnp.bfloat16))
    tall = jnp.concatenate(pieces, axis=0)
    tall = jnp.concatenate([tall, tall], axis=1)
    for t in range(terms):
        mixed = dot_over(tall, left_mix_ref[t], 1, 0).astype(jnp.bfloat16)
        for b in range(len(pieces)):
            gated[
                t * states : (t + 1) * states, out_first + b * wide : out_first + (b + 1) * wide
            ] = mixed[b * states : (b + 1) * states, :]


def gate_sector(row, live, left_refs, left_mix, gated):
    chunks = len(left_refs)
    chunk_rows = left_refs[0].shape[0]
    for c in range(chunks):
        first_row = lax.rem(row + (chunks - c), chunks) * chunk_rows
        gate_chunk(left_refs[c], live, first_row, left_mix, gated, c * chunk_rows)
    return two_parts(dot_over(gated[...], gated[...], 1, 1))


def place(place_ref, rows, slots, sectors):
    row = lax.rem(place_ref[0], rows)
    right_first = lax.div(place_ref[0], rows) * slots
    return row, lax.rem(right_first + sectors // 2, sectors), right_first


def weight_of(charges_ref, sector):
    charge = charges_ref[sector].astype(jnp.float32)
    return jnp.exp(jnp.full((1, 1), -chemical * charge, jnp.float32))


def left_kernel(slots, place_ref, live_ref, left_ops_ref, *refs):
    left_refs = refs[:-5]
    row, left_first, _ = place(place_ref, len(left_refs), slots, live_ref.shape[0])
    own_ref, high_ref, low_ref, left_mix, gated = refs[-5:]
    build_left_mix(left_ops_ref, left_mix)
    high_ref[...], low_ref[...] = gate_sector(
        row, live_ref[left_first], left_refs, left_mix, gated
    )
    own_ref[...] = gated[:, : own_ref.shape[1]]


def krylov_kernel(place_ref, live_ref, kept_ref, charges_ref, *refs):
    chunks = len(refs) - 16
    left_refs = refs[:chunks]
    (left_mix, first_own, first_high, first_low, start_ref) = refs[chunks : chunks + 5]
    square_refs = refs[chunks + 5 : chunks + 9]
    (basis_ref, image_ref) = refs[chunks + 9 : chunks + 11]
    (gated, second_high, second_low, block, final) = refs[chunks + 11 :]
    slots, keep, bond = image_ref.shape
    chunk_rows = left_refs[0].shape[0]
    row, left_first, right_first = place(place_ref, chunks, slots, live_ref.shape[0])
    second_high[...], second_low[...] = gate_sector(
        row, live_ref[left_first + 1], left_refs, left_mix, gated
    )
    gram_refs = ((first_high, first_low), (second_high, second_low))
    for s in range(slots):
        columns = start_ref[pl.ds(left_first + s, 1), :].astype(jnp.float32)
        columns = jnp.broadcast_to(columns, (8, keep)).T[:, :1]
        spots = lax.broadcasted_iota(jnp.int32, (keep, bond), 1).astype(jnp.float32)
        block[s] = jnp.where(spots == columns, 1.0, 0.0)
    weights = [weight_of(charges_ref, right_first + s) for s in range(slots)]

    def step(index, carry):
        images = [
            three_pass(two_parts(block[s]), (gram_refs[s][0][...], gram_refs[s][1][...]), 0)
            for s in range(slots)
        ]
        grams = [dot_over(images[s], block[s], 1, 1, highest) for s in range(slots)]
        inverses = [two_parts(inverse) for inverse in lower_inverse(grams, WINDOW)]
        for s in range(slots):
            image_ref[s] = three_pass(inverses[s], two_parts(images[s]), 0)

        @pl.when(index == ITERS)
        def _():
            for s in range(slots):
                final[s] = three_pass(inverses[s], two_parts(block[s]), 0)

        @pl.when(index < ITERS)
        def _():
            for s in range(slots):
                squares = (square_refs[2 * s][...], square_refs[2 * s + 1][...])
                scale = weights[s] * weights[s]
                block[s] = scale * three_pass(two_parts(image_ref[s]), squares, 0)

        return carry

    lax.fori_loop(0, ITERS + 1, step, 0)
    for s, rows in enumerate((first_own[...], gated[:, :chunk_rows])):
        high, low = two_parts(final[s])
        basis = dot_over(high, rows, 1, 0) + dot_over(low, rows, 1, 0)
        keeps = lax.broadcasted_iota(jnp.int32, basis.shape, 0) < kept_ref[right_first + s]
        basis_ref[s] = jnp.where(keeps, basis, 0.0).T.astype(jnp.bfloat16)


def truncate_kernel(rows, place_ref, kept_ref, charges_ref, image_ref, *refs):
    _, _, right_first = place(place_ref, rows, image_ref.shape[0], kept_ref.shape[0])
    square_refs, local_refs, (right_ref, total_ref) = refs[:4], refs[4:6], refs[6:]
    total = jnp.zeros((1, 1), jnp.float32)
    for s in range(image_ref.shape[0]):
        image = image_ref[s]
        high, low = two_parts(image)
        kept = kept_ref[right_first + s]
        weight = weight_of(charges_ref, right_first + s)
        keeps = lax.broadcasted_iota(jnp.int32, image.shape, 0) < kept
        scale = weight * weight
        squares = (square_refs[2 * s][...], square_refs[2 * s + 1][...])
        squared = scale * three_pass((high, low), squares, 0) * image
        squared = jnp.where(keeps, squared, 0.0)
        total += jnp.sum(jnp.sum(squared, axis=0, keepdims=True), axis=1, keepdims=True)
        local = local_refs[s][...]
        part = dot_over(high, local, 1, 0) + dot_over(low, local, 1, 0)
        keeps = lax.broadcasted_iota(jnp.int32, part.shape, 0) < kept
        right_ref[s] = jnp.where(keeps, part * weight, 0.0)
    total_ref[...] = jnp.broadcast_to(total, total_ref.shape)


def finish_kernel(totals_ref, part_ref, sent_ref, basis_ref, right_ref):
    basis_ref[...] = sent_ref[...].astype(jnp.float32)
    total = jnp.sum(totals_ref[...], axis=0, keepdims=True)[:, :1]
    factor = 1.0 / jnp.sqrt(total)
    for s in range(part_ref.shape[0]):
        right_ref[s] = part_ref[s] * factor


def smem():
    return pl.BlockSpec(memory_space=pltpu.SMEM)


def vmem():
    return pl.BlockSpec(memory_space=pltpu.VMEM)


def shape_of(shape, dtype):
    return jax.ShapeDtypeStruct(shape, dtype)


def kernel_options(mebibytes, flops):
    return dict(
        compiler_params=pltpu.CompilerParams(vmem_limit_bytes=mebibytes << 20),
        cost_estimate=pl.CostEstimate(flops=int(flops), bytes_accessed=2 << 20, transcendentals=0),
    )


def gate_right(slot, row, right_block, right_ops, local_cols):
    _, states, cols = right_block.shape
    terms = right_ops.shape[0]
    bond, wide = terms * states, SITE * SITE
    return pl.pallas_call(
        functools.partial(right_kernel, slot, cols // local_cols),
        in_specs=[smem(), pl.BlockSpec(memory_space=pltpu.HBM), vmem()],
        out_specs=[vmem()] * 3,
        out_shape=[
            shape_of((bond, bond), jnp.bfloat16),
            shape_of((bond, bond), jnp.bfloat16),
            shape_of((bond, local_cols), jnp.bfloat16),
        ],
        scratch_shapes=[
            pltpu.VMEM((terms * wide, 2 * wide), jnp.bfloat16),
            pltpu.VMEM((bond, cols), jnp.bfloat16),
            pltpu.VMEM((states, cols), jnp.bfloat16),
            pltpu.SemaphoreType.DMA,
        ],
        name="right_gate",
        **kernel_options(12, 4e9),
    )(row, right_block, right_ops.reshape(terms * SITE, SITE))


def gate_left(slots, row, live, left_chunks, left_ops):
    chunk_rows, states = left_chunks[0].shape
    terms = left_ops.shape[0]
    bond, wide = terms * states, SITE * SITE
    return pl.pallas_call(
        functools.partial(left_kernel, slots),
        in_specs=[smem()] * 2 + [vmem()] * (1 + len(left_chunks)),
        out_specs=[vmem()] * 4,
        out_shape=[
            shape_of((bond, chunk_rows), jnp.bfloat16),
            shape_of((bond, bond), jnp.bfloat16),
            shape_of((bond, bond), jnp.bfloat16),
            shape_of((terms, 2 * wide, wide), jnp.bfloat16),
        ],
        scratch_shapes=[pltpu.VMEM((bond, len(left_chunks) * chunk_rows), jnp.bfloat16)],
        name="left_gate",
        **kernel_options(10, 4e9),
    )(row, live, left_ops, *left_chunks)


def krylov_part(slots, row, live, kept, charges, left_chunks, left_mix, first, start, squares):
    chunk_rows, _ = left_chunks[0].shape
    bond = squares[0].shape[0]
    keep = start.shape[1]
    return pl.pallas_call(
        krylov_kernel,
        in_specs=[smem()] * 4 + [vmem()] * (len(left_chunks) + 2 + len(first) + len(squares)),
        out_specs=[vmem()] * 2,
        out_shape=[
            shape_of((slots, chunk_rows, keep), jnp.bfloat16),
            shape_of((slots, keep, bond), jnp.float32),
        ],
        scratch_shapes=[
            pltpu.VMEM((bond, len(left_chunks) * chunk_rows), jnp.bfloat16),
            pltpu.VMEM((bond, bond), jnp.bfloat16),
            pltpu.VMEM((bond, bond), jnp.bfloat16),
            pltpu.VMEM((slots, keep, bond), jnp.float32),
            pltpu.VMEM((slots, keep, bond), jnp.float32),
        ],
        name="krylov",
        **kernel_options(14, 2e10),
    )(row, live, kept, charges, *left_chunks, left_mix, *first, start, *squares)


def truncated(rows, row, kept, charges, image, squares, locals_, peers):
    slots, keep, _ = image.shape
    local_cols = locals_[0].shape[1]
    return pl.pallas_call(
        functools.partial(truncate_kernel, rows),
        in_specs=[smem()] * 3 + [vmem()] * (1 + len(squares) + len(locals_)),
        out_specs=[vmem()] * 2,
        out_shape=[
            shape_of((slots, keep, local_cols), jnp.float32),
            shape_of((peers, keep), jnp.float32),
        ],
        name="truncate",
        **kernel_options(8, 2e9),
    )(row, kept, charges, image, *squares, *locals_)


def finished(totals, part, sent):
    return pl.pallas_call(
        finish_kernel,
        in_specs=[vmem()] * 3,
        out_specs=[vmem()] * 2,
        out_shape=[shape_of(sent.shape, jnp.float32), shape_of(part.shape, jnp.float32)],
        name="finish",
        **kernel_options(4, 1e6),
    )(totals, part, sent)


def on_device(left_block, right_block, left_ops, right_ops, charges, live_states, kept, start):
    slots = left_block.shape[0]
    top_bit = lax.axis_size(SEC).bit_length() - 2
    row = lax.axis_index(SEC_ROW).astype(jnp.int32).reshape(1)
    local_cols = right_block.shape[2] // lax.axis_size("row")
    rows = lax.axis_size("row")

    def over_rows(chunk):
        sent = [
            lax.ppermute(chunk, "row", [(i, (i + d) % rows) for i in range(rows)])
            for d in range(1, rows)
        ]
        return [chunk, *sent]

    theirs = [from_partner(left_block[0], SEC, top_bit)]
    first = list(gate_right(0, row, right_block, right_ops, local_cols))
    second_block, first[0] = lax.optimization_barrier((left_block[1], first[0]))
    theirs.append(from_partner(second_block, SEC, top_bit))
    theirs[0], first[0], row_second = lax.optimization_barrier((theirs[0], first[0], row))
    first_chunks = over_rows(theirs[0])
    second = list(gate_right(1, row_second, right_block, right_ops, local_cols))
    theirs[1], second[0], row_left = lax.optimization_barrier((theirs[1], second[0], row))
    second_chunks = over_rows(theirs[1])
    *first_left, left_mix = gate_left(slots, row_left, live_states, first_chunks, left_ops)
    squares = (*first[:2], *second[:2])
    basis, image = krylov_part(
        slots, row, live_states, kept, charges, second_chunks, left_mix, first_left, start, squares
    )
    basis = from_partner(basis, SEC, top_bit)
    right_part, total = truncated(
        rows, row, kept, charges, image, squares, (first[2], second[2]), lax.axis_size(SEC)
    )
    totals = lax.all_to_all(total, SEC, split_axis=0, concat_axis=0, tiled=True)
    return tuple(finished(totals, right_part, basis))


def solution(mesh):
    finer = Mesh(
        mesh.devices.reshape(8, 4, 2, mesh.shape["row"]), ("sec_0", "sec_1", "sec_2", "row")
    )
    in_specs = (P(SEC, "row", None), P(SEC, None, None), P(), P(), P(), P(), P(), P())
    out_specs = (P(SEC, "row", None), P(SEC, None, "row"))
    return jax.shard_map(
        on_device, mesh=finer, in_specs=in_specs, out_specs=out_specs, check_vma=False
    )
```

```python
import functools

import jax
import jax.numpy as jnp
from jax import lax
from jax.experimental import pallas as pl
from jax.experimental.pallas import tpu as pltpu
from jax.sharding import Mesh
from jax.sharding import PartitionSpec as P

SITE = 16
ITERS = 2
SEC = ("sec_0", "sec_1", "sec_2")
SEC_ROW = ("sec_0", "sec_1", "sec_2", "row")
WINDOW = 32

chemical = 0.4
highest = lax.Precision.HIGHEST


def from_partner(value, axis, distance):
    mask = 2**distance
    pairs = [(source, source ^ mask) for source in range(lax.axis_size(axis))]
    return lax.ppermute(value, axis, pairs)


def dot_over(left, right, left_dim, right_dim, precision=None):
    return lax.dot_general(
        left,
        right,
        (((left_dim,), (right_dim,)), ((), ())),
        precision=precision,
        preferred_element_type=jnp.float32,
    )


def two_parts(values):
    high = values.astype(jnp.bfloat16)
    low = (values - high.astype(jnp.float32)).astype(jnp.bfloat16)
    return high, low


def one_hot(shape, row_key, col_key):
    rows = lax.broadcasted_iota(jnp.int32, shape, 0)
    cols = lax.broadcasted_iota(jnp.int32, shape, 1)
    return row_key(rows) == col_key(cols)


def as_weights(mask):
    return jnp.where(mask, 1.0, 0.0).astype(jnp.bfloat16)


def lower_inverse(grams, window):
    n = grams[0].shape[0]
    lane = lax.broadcasted_iota(jnp.int32, (8, n), 1)
    sub = lax.broadcasted_iota(jnp.int32, (8, n), 0)
    spots = [jnp.full((8, n), m, jnp.int32) for m in range(8)]
    rows = [[g[8 * q : 8 * q + 8, :] for q in range(n // 8)] for g in grams]
    span = window // 8
    for first in range(0, n // 8, span):
        last = first + span
        for q in range(first, last):
            k = 8 * q
            inside = (lane >= k) & (lane < k + 8)
            unit = (lane - k == sub).astype(jnp.float32)
            for mat in rows:
                cols = {
                    r: [jnp.take_along_axis(mat[r], spots[m] + k, axis=1) for m in range(8)]
                    for r in range(q, last)
                }
                for r in range(q, last):
                    mat[r] = jnp.where(inside, unit if r == q else 0.0, mat[r])
                pivot = jnp.broadcast_to(cols[q][0][0:1, :], (8, n))
                for m in range(8):
                    scale = lax.rsqrt(pivot)
                    weights = {
                        j: jnp.broadcast_to(cols[q][m][j : j + 1, :], (8, n)) * scale
                        for j in range(m + 1, 8)
                    }
                    if m < 7:
                        ahead = jnp.broadcast_to(cols[q][m + 1][m + 1 : m + 2, :], (8, n))
                        pivot = ahead - weights[m + 1] * weights[m + 1]
                    below = {r: cols[r][m] * scale for r in range(q, last)}
                    head = jnp.broadcast_to(mat[q][m : m + 1, :], (8, n)) * scale
                    for j in range(m + 1, 8):
                        for r in range(q, last):
                            cols[r][j] = cols[r][j] - below[r] * weights[j]
                    below[q] = jnp.where(sub > m, below[q], 0.0)
                    for r in range(q, last):
                        mat[r] = mat[r] - below[r] * head
                    mat[q] = jnp.where(sub == m, head, mat[q])
        if last < n // 8:
            inblock = (lane >= 8 * first) & (lane < 8 * last)
            for mat in rows:
                panel = jnp.concatenate(mat[first:last], axis=0)
                panel_row = lax.broadcasted_iota(jnp.int32, panel.shape, 0) + 8 * first
                panel_lane = lax.broadcasted_iota(jnp.int32, panel.shape, 1)
                panel = jnp.where((panel_lane > panel_row) & (panel_lane < 8 * last), 0.0, panel)
                update = dot_over(panel, panel, 0, 0, highest)
                for r in range(last, n // 8):
                    mat[r] = jnp.where(inblock, 0.0, mat[r]) - update[8 * r : 8 * r + 8, :]
    full_row = lax.broadcasted_iota(jnp.int32, (n, n), 0)
    full_col = lax.broadcasted_iota(jnp.int32, (n, n), 1)
    return [jnp.where(full_col <= full_row, jnp.concatenate(mat, axis=0), 0.0) for mat in rows]


def three_pass(left, right, right_dim):
    (left_high, left_low), (right_high, right_low) = left, right
    return (
        dot_over(left_high, right_high, 1, right_dim)
        + dot_over(left_high, right_low, 1, right_dim)
        + dot_over(left_low, right_high, 1, right_dim)
    )


def right_kernel(
    slot, rows, build, place_ref, right_ref, given_ref, high_ref, low_ref, local_ref, *refs
):
    *made, gated, right, sem = refs
    right_mix = made[0] if build else given_ref
    states = right.shape[0]
    terms = gated.shape[0] // states
    wide = SITE * SITE
    local_cols = local_ref.shape[1]
    fetch = pltpu.make_async_copy(right_ref.at[slot], right, sem)
    fetch.start()
    if build:
        spread = as_weights(one_hot((terms * wide, terms * SITE), lambda r: r // SITE, lambda c: c))
        widen = as_weights(one_hot((SITE, wide), lambda r: r, lambda c: c // SITE))
        same = one_hot((terms * wide, wide), lambda r: r % SITE, lambda c: c % SITE)
        for part, piece in enumerate(two_parts(given_ref[...])):
            tall = dot_over(spread, piece, 1, 0).astype(jnp.bfloat16)
            full = dot_over(tall, widen, 1, 0)
            right_mix[:, part * wide : (part + 1) * wide] = jnp.where(same, full, 0.0).astype(
                jnp.bfloat16
            )
    fetch.wait()
    for pair in range(states // (2 * SITE)):
        base = pair * 2 * SITE
        halves = [
            jnp.concatenate(
                [
                    right[base + h * SITE : base + (h + 1) * SITE, j * states : (j + 1) * states]
                    for j in range(SITE)
                ],
                axis=0,
            )
            for h in range(2)
        ]
        block = jnp.concatenate(halves, axis=1)
        block = jnp.concatenate([block, block], axis=0)
        for t in range(terms):
            mixed = dot_over(right_mix[t * wide : (t + 1) * wide, :], block, 1, 0)
            mixed = mixed.astype(jnp.bfloat16)
            for h in range(2):
                for i in range(SITE):
                    gated[
                        t * states + base + h * SITE : t * states + base + (h + 1) * SITE,
                        i * states : (i + 1) * states,
                    ] = mixed[i * SITE : (i + 1) * SITE, h * states : (h + 1) * states]
    high_ref[...], low_ref[...] = two_parts(dot_over(gated[...], gated[...], 1, 1))
    offset = pl.multiple_of(lax.rem(place_ref[0], rows) * local_cols, local_cols)
    local_ref[...] = gated[:, pl.ds(offset, local_cols)]


def build_left_mix(left_ops_ref, left_mix):
    terms, _, wide = left_mix.shape
    tall_pick = as_weights(one_hot((wide, SITE), lambda r: r % SITE, lambda c: c))
    wide_pick = as_weights(one_hot((SITE, wide), lambda r: r, lambda c: c % SITE))
    group = one_hot((wide, wide), lambda r: r // SITE, lambda c: c // SITE)
    for t in range(terms):
        for part, piece in enumerate(two_parts(left_ops_ref[t])):
            tall = dot_over(tall_pick, piece, 1, 1).astype(jnp.bfloat16)
            full = dot_over(tall, wide_pick, 1, 0)
            left_mix[t, part * wide : (part + 1) * wide, :] = jnp.where(group, full, 0.0).astype(
                jnp.bfloat16
            )


def gate_chunk(left_ref, live, first_row, left_mix_ref, gated, out_first):
    chunk_rows, states = left_ref.shape
    terms, _, wide = left_mix_ref.shape
    turned = left_ref[...].T
    pieces = []
    for b in range(chunk_rows // wide):
        lane = lax.broadcasted_iota(jnp.int32, (states, wide), 1)
        alive = lane < live * SITE - (first_row + b * wide)
        piece = turned[:, b * wide : (b + 1) * wide].astype(jnp.float32)
        pieces.append(jnp.where(alive, piece, 0.0).astype(jnp.bfloat16))
    tall = jnp.concatenate(pieces, axis=0)
    tall = jnp.concatenate([tall, tall], axis=1)
    for t in range(terms):
        mixed = dot_over(tall, left_mix_ref[t], 1, 0).astype(jnp.bfloat16)
        for b in range(len(pieces)):
            gated[
                t * states : (t + 1) * states, out_first + b * wide : out_first + (b + 1) * wide
            ] = mixed[b * states : (b + 1) * states, :]


def gate_sector(row, live, left_refs, left_mix, gated):
    chunks = len(left_refs)
    chunk_rows = left_refs[0].shape[0]
    for c in range(chunks):
        first_row = lax.rem(row + (chunks - c), chunks) * chunk_rows
        gate_chunk(left_refs[c], live, first_row, left_mix, gated, c * chunk_rows)
    return two_parts(dot_over(gated[...], gated[...], 1, 1))


def place(place_ref, rows, slots, sectors):
    row = lax.rem(place_ref[0], rows)
    right_first = lax.div(place_ref[0], rows) * slots
    return row, lax.rem(right_first + sectors // 2, sectors), right_first


def weight_of(charges_ref, sector):
    charge = charges_ref[sector].astype(jnp.float32)
    return jnp.exp(jnp.full((1, 1), -chemical * charge, jnp.float32))


def left_kernel(slots, place_ref, live_ref, left_ops_ref, *refs):
    left_refs = refs[:-5]
    row, left_first, _ = place(place_ref, len(left_refs), slots, live_ref.shape[0])
    own_ref, high_ref, low_ref, left_mix, gated = refs[-5:]
    build_left_mix(left_ops_ref, left_mix)
    high_ref[...], low_ref[...] = gate_sector(
        row, live_ref[left_first], left_refs, left_mix, gated
    )
    own_ref[...] = gated[:, : own_ref.shape[1]]


def krylov_kernel(place_ref, live_ref, kept_ref, charges_ref, *refs):
    chunks = len(refs) - 16
    left_refs = refs[:chunks]
    (left_mix, first_own, first_high, first_low, start_ref) = refs[chunks : chunks + 5]
    square_refs = refs[chunks + 5 : chunks + 9]
    (basis_ref, image_ref) = refs[chunks + 9 : chunks + 11]
    (gated, second_high, second_low, block, final) = refs[chunks + 11 :]
    slots, keep, bond = image_ref.shape
    chunk_rows = left_refs[0].shape[0]
    row, left_first, right_first = place(place_ref, chunks, slots, live_ref.shape[0])
    second_high[...], second_low[...] = gate_sector(
        row, live_ref[left_first + 1], left_refs, left_mix, gated
    )
    gram_refs = ((first_high, first_low), (second_high, second_low))
    for s in range(slots):
        columns = start_ref[pl.ds(left_first + s, 1), :].astype(jnp.float32)
        columns = jnp.broadcast_to(columns, (8, keep)).T[:, :1]
        spots = lax.broadcasted_iota(jnp.int32, (keep, bond), 1).astype(jnp.float32)
        block[s] = jnp.where(spots == columns, 1.0, 0.0)
    weights = [weight_of(charges_ref, right_first + s) for s in range(slots)]

    def step(index, carry):
        images = [
            three_pass(two_parts(block[s]), (gram_refs[s][0][...], gram_refs[s][1][...]), 0)
            for s in range(slots)
        ]
        grams = [dot_over(images[s], block[s], 1, 1, highest) for s in range(slots)]
        inverses = [two_parts(inverse) for inverse in lower_inverse(grams, WINDOW)]
        for s in range(slots):
            image_ref[s] = three_pass(inverses[s], two_parts(images[s]), 0)

        @pl.when(index == ITERS)
        def _():
            for s in range(slots):
                final[s] = three_pass(inverses[s], two_parts(block[s]), 0)

        @pl.when(index < ITERS)
        def _():
            for s in range(slots):
                squares = (square_refs[2 * s][...], square_refs[2 * s + 1][...])
                scale = weights[s] * weights[s]
                block[s] = scale * three_pass(two_parts(image_ref[s]), squares, 0)

        return carry

    lax.fori_loop(0, ITERS + 1, step, 0)
    for s, rows in enumerate((first_own[...], gated[:, :chunk_rows])):
        high, low = two_parts(final[s])
        basis = dot_over(high, rows, 1, 0) + dot_over(low, rows, 1, 0)
        keeps = lax.broadcasted_iota(jnp.int32, basis.shape, 0) < kept_ref[right_first + s]
        basis_ref[s] = jnp.where(keeps, basis, 0.0).T.astype(jnp.bfloat16)


def truncate_kernel(rows, place_ref, kept_ref, charges_ref, image_ref, *refs):
    _, _, right_first = place(place_ref, rows, image_ref.shape[0], kept_ref.shape[0])
    square_refs, local_refs, (right_ref, total_ref) = refs[:4], refs[4:6], refs[6:]
    total = jnp.zeros((1, 1), jnp.float32)
    for s in range(image_ref.shape[0]):
        image = image_ref[s]
        high, low = two_parts(image)
        kept = kept_ref[right_first + s]
        weight = weight_of(charges_ref, right_first + s)
        keeps = lax.broadcasted_iota(jnp.int32, image.shape, 0) < kept
        scale = weight * weight
        squares = (square_refs[2 * s][...], square_refs[2 * s + 1][...])
        squared = scale * three_pass((high, low), squares, 0) * image
        squared = jnp.where(keeps, squared, 0.0)
        total += jnp.sum(jnp.sum(squared, axis=0, keepdims=True), axis=1, keepdims=True)
        local = local_refs[s][...]
        part = dot_over(high, local, 1, 0) + dot_over(low, local, 1, 0)
        keeps = lax.broadcasted_iota(jnp.int32, part.shape, 0) < kept
        right_ref[s] = jnp.where(keeps, part * weight, 0.0)
    total_ref[...] = jnp.broadcast_to(total, total_ref.shape)


def finish_kernel(totals_ref, part_ref, sent_ref, basis_ref, right_ref):
    basis_ref[...] = sent_ref[...].astype(jnp.float32)
    total = jnp.sum(totals_ref[...], axis=0, keepdims=True)[:, :1]
    factor = 1.0 / jnp.sqrt(total)
    for s in range(part_ref.shape[0]):
        right_ref[s] = part_ref[s] * factor


def smem():
    return pl.BlockSpec(memory_space=pltpu.SMEM)


def vmem():
    return pl.BlockSpec(memory_space=pltpu.VMEM)


def shape_of(shape, dtype):
    return jax.ShapeDtypeStruct(shape, dtype)


def kernel_options(mebibytes, flops):
    return dict(
        compiler_params=pltpu.CompilerParams(vmem_limit_bytes=mebibytes << 20),
        cost_estimate=pl.CostEstimate(flops=int(flops), bytes_accessed=2 << 20, transcendentals=0),
    )


def gate_right(slot, row, right_block, given, local_cols, build):
    _, states, cols = right_block.shape
    wide = SITE * SITE
    terms = given.shape[0] // (SITE if build else wide)
    bond = terms * states
    made = [shape_of((terms * wide, 2 * wide), jnp.bfloat16)] if build else []
    return pl.pallas_call(
        functools.partial(right_kernel, slot, cols // local_cols, build),
        in_specs=[smem(), pl.BlockSpec(memory_space=pltpu.HBM), vmem()],
        out_specs=[vmem()] * (3 + len(made)),
        out_shape=[
            shape_of((bond, bond), jnp.bfloat16),
            shape_of((bond, bond), jnp.bfloat16),
            shape_of((bond, local_cols), jnp.bfloat16),
            *made,
        ],
        scratch_shapes=[
            pltpu.VMEM((bond, cols), jnp.bfloat16),
            pltpu.VMEM((states, cols), jnp.bfloat16),
            pltpu.SemaphoreType.DMA,
        ],
        name="right_gate",
        **kernel_options(12, 4e9),
    )(row, right_block, given)


def gate_left(slots, row, live, left_chunks, left_ops):
    chunk_rows, states = left_chunks[0].shape
    terms = left_ops.shape[0]
    bond, wide = terms * states, SITE * SITE
    return pl.pallas_call(
        functools.partial(left_kernel, slots),
        in_specs=[smem()] * 2 + [vmem()] * (1 + len(left_chunks)),
        out_specs=[vmem()] * 4,
        out_shape=[
            shape_of((bond, chunk_rows), jnp.bfloat16),
            shape_of((bond, bond), jnp.bfloat16),
            shape_of((bond, bond), jnp.bfloat16),
            shape_of((terms, 2 * wide, wide), jnp.bfloat16),
        ],
        scratch_shapes=[pltpu.VMEM((bond, len(left_chunks) * chunk_rows), jnp.bfloat16)],
        name="left_gate",
        **kernel_options(10, 4e9),
    )(row, live, left_ops, *left_chunks)


def krylov_part(slots, row, live, kept, charges, left_chunks, left_mix, first, start, squares):
    chunk_rows, _ = left_chunks[0].shape
    bond = squares[0].shape[0]
    keep = start.shape[1]
    return pl.pallas_call(
        krylov_kernel,
        in_specs=[smem()] * 4 + [vmem()] * (len(left_chunks) + 2 + len(first) + len(squares)),
        out_specs=[vmem()] * 2,
        out_shape=[
            shape_of((slots, chunk_rows, keep), jnp.bfloat16),
            shape_of((slots, keep, bond), jnp.float32),
        ],
        scratch_shapes=[
            pltpu.VMEM((bond, len(left_chunks) * chunk_rows), jnp.bfloat16),
            pltpu.VMEM((bond, bond), jnp.bfloat16),
            pltpu.VMEM((bond, bond), jnp.bfloat16),
            pltpu.VMEM((slots, keep, bond), jnp.float32),
            pltpu.VMEM((slots, keep, bond), jnp.float32),
        ],
        name="krylov",
        **kernel_options(14, 2e10),
    )(row, live, kept, charges, *left_chunks, left_mix, *first, start, *squares)


def truncated(rows, row, kept, charges, image, squares, locals_, peers):
    slots, keep, _ = image.shape
    local_cols = locals_[0].shape[1]
    return pl.pallas_call(
        functools.partial(truncate_kernel, rows),
        in_specs=[smem()] * 3 + [vmem()] * (1 + len(squares) + len(locals_)),
        out_specs=[vmem()] * 2,
        out_shape=[
            shape_of((slots, keep, local_cols), jnp.float32),
            shape_of((peers, keep), jnp.float32),
        ],
        name="truncate",
        **kernel_options(8, 2e9),
    )(row, kept, charges, image, *squares, *locals_)


def finished(totals, part, sent):
    return pl.pallas_call(
        finish_kernel,
        in_specs=[vmem()] * 3,
        out_specs=[vmem()] * 2,
        out_shape=[shape_of(sent.shape, jnp.float32), shape_of(part.shape, jnp.float32)],
        name="finish",
        **kernel_options(4, 1e6),
    )(totals, part, sent)


def on_device(left_block, right_block, left_ops, right_ops, charges, live_states, kept, start):
    slots = left_block.shape[0]
    top_bit = lax.axis_size(SEC).bit_length() - 2
    row = lax.axis_index(SEC_ROW).astype(jnp.int32).reshape(1)
    local_cols = right_block.shape[2] // lax.axis_size("row")
    rows = lax.axis_size("row")

    def over_rows(chunk):
        sent = [
            lax.ppermute(chunk, "row", [(i, (i + d) % rows) for i in range(rows)])
            for d in range(1, rows)
        ]
        return [chunk, *sent]

    theirs = [from_partner(left_block[0], SEC, top_bit)]
    factors = right_ops.reshape(-1, SITE)
    *first, right_mix = gate_right(0, row, right_block, factors, local_cols, True)
    second_block, first[0] = lax.optimization_barrier((left_block[1], first[0]))
    theirs.append(from_partner(second_block, SEC, top_bit))
    theirs[0], first[0], row_second = lax.optimization_barrier((theirs[0], first[0], row))
    first_chunks = over_rows(theirs[0])
    second = list(gate_right(1, row_second, right_block, right_mix, local_cols, False))
    theirs[1], second[0], row_left = lax.optimization_barrier((theirs[1], second[0], row))
    second_chunks = over_rows(theirs[1])
    *first_left, left_mix = gate_left(slots, row_left, live_states, first_chunks, left_ops)
    squares = (*first[:2], *second[:2])
    basis, image = krylov_part(
        slots, row, live_states, kept, charges, second_chunks, left_mix, first_left, start, squares
    )
    basis = from_partner(basis, SEC, top_bit)
    right_part, total = truncated(
        rows, row, kept, charges, image, squares, (first[2], second[2]), lax.axis_size(SEC)
    )
    totals = lax.all_to_all(total, SEC, split_axis=0, concat_axis=0, tiled=True)
    return tuple(finished(totals, right_part, basis))


def solution(mesh):
    finer = Mesh(
        mesh.devices.reshape(8, 4, 2, mesh.shape["row"]), ("sec_0", "sec_1", "sec_2", "row")
    )
    in_specs = (P(SEC, "row", None), P(SEC, None, None), P(), P(), P(), P(), P(), P())
    out_specs = (P(SEC, "row", None), P(SEC, None, "row"))
    return jax.shard_map(
        on_device, mesh=finer, in_specs=in_specs, out_specs=out_specs, check_vma=False
    )
```
